32 devices in a mesh: tok: 8 (over z, x), head: 4 (over y, core).
Axes of the slice: x: 2, y: 2, z: 4, core: 2. Of those that a mesh axis runs over, the one named last changes fastest.
Arguments:
- queries: bfloat16 [2048, 8192], P(('tok', 'head')), may hold values from -6 to 6
- keys: bfloat16 [2048, 1024], P(('tok', 'head')), may hold values from -6 to 6
- values: bfloat16 [2048, 1024], P(('tok', 'head')), may hold values from -6 to 6
- doc_ids: int32 [2048], replicated, may hold values from 0 to 2, never falling along the last dimension, each value on 1 to 1792 neighbouring positions
Outputs:
- attention: bfloat16 [2048, 8192], P('tok', 'head')
The draws below stay inside these ranges and needn't reach their ends.
Inputs may be any that keep to these rules, and one draw needn't show every extreme that they name: doc_ids never falls along the tokens; each document holds 1 to 1792 tokens and some document holds exactly 1792.
All inputs are finite; a program needn't handle non-finite values.
Results may differ from the reference program's by a relative error of at most 0.0038.
Values may be sent and summed in bfloat16 or wider, within the bound.
A program may use at most 64 MiB of HBM per device.

```python
import math
import jax
import jax.numpy as jnp
import numpy as np
from jax import lax

QH = 64
KVH = 8
HD = 128
TOK_DEV = 256
REACH = 7
TOKENS = 2048
DOC_MAX = 1792
DOCS = 3


def draw_queries(key, part):
    base = jax.random.truncated_normal(jax.random.fold_in(key, 1), -6.0, 6.0, (TOKENS, QH * HD), jnp.float32)
    return base.astype(jnp.bfloat16)


def draw_keys(key, part):
    base = jax.random.truncated_normal(jax.random.fold_in(key, 2), -6.0, 6.0, (TOKENS, KVH * HD), jnp.float32)
    return base.astype(jnp.bfloat16)


def steps_of(own_key, dims, pieces, low, top_value):
    level, own = 1.0, jax.random.fold_in(own_key, 6)
    for position, blocks in pieces:
        heights = jnp.exp(jax.random.uniform(jax.random.fold_in(own, position), (blocks,), jnp.float32, low / len(pieces), top_value / len(pieces)))
        level = level * jnp.repeat(heights, dims[position] // blocks).reshape([-1 if axis == position else 1 for axis in range(len(dims))])
    return level


def split_up(number_of, total, limit, skew):
    loads = [(1 << 20) // math.isqrt(rank ** skew) + 1 for rank in range(2, number_of + 1)]
    spare, given = total - limit - (number_of - 1), [1] * (number_of - 1)
    while spare > 0:
        candidates = [i for i in range(number_of - 1) if given[i] < limit]
        pool, left = sum([loads[i] for i in candidates]), spare
        for i in candidates:
            addition = min(limit - given[i], max(1, left * loads[i] // pool), spare)
            given[i] = given[i] + addition
            spare = spare - addition
    return np.array([limit] + given)


def uneven_parts(stream_key, count, total, most, lean):
    if count == 2:
        one = jax.random.randint(stream_key, (), max(1, total - most), min(most, total - 1) + 1)
        return jnp.stack([one, total - one])
    tallies = jnp.asarray(split_up(count, total, most, lean), jnp.int32)
    twos = (count - 1) // 2
    source_of, sink = tallies[1:1 + 2 * twos:2], tallies[2:2 + 2 * twos:2]
    room = jnp.minimum(source_of - 1, most - sink)
    shifted = jax.random.randint(jax.random.fold_in(stream_key, 1), (twos,), 0, 1 << 20) % (room + 1)
    tallies = tallies.at[1:1 + 2 * twos:2].set(source_of - shifted).at[2:2 + 2 * twos:2].set(sink + shifted)
    return tallies[jax.random.permutation(jax.random.fold_in(stream_key, 2), count)]


def bell_draw(rng, dims, scale, reach, split=(), kind=jnp.bfloat16):
    values = scale * jax.random.normal(rng, dims, jnp.float32)
    if split:
        values = values * steps_of(rng, dims, split, -0.22, 0.18)
    return jnp.clip(values, -reach, reach).astype(kind)


def setup_inputs(seed: int = 0) -> dict:
    arg_keys = jax.random.split(jax.random.key(seed), 5)
    return {
        "queries": draw_queries(jax.random.fold_in(arg_keys[4], 71), 0),
        "keys": draw_keys(jax.random.fold_in(arg_keys[4], 71), 0),
        "values": bell_draw(arg_keys[2], (TOKENS, KVH * HD), 1.0, 6.0, ((0, 32),)),
        "doc_ids": jnp.searchsorted(jnp.cumsum(uneven_parts(arg_keys[3], DOCS, TOKENS, DOC_MAX, 2)), jnp.arange(TOKENS), side="right").astype(jnp.int32),
    }


def reference(queries, keys, values, doc_ids):
    groups = QH // KVH
    extent = REACH * TOK_DEV
    window = extent + TOK_DEV
    scaling = HD ** -0.5
    key_pad = jnp.concatenate([jnp.zeros((extent, KVH * HD), keys.dtype), keys], axis=0)
    value_pad = jnp.concatenate([jnp.zeros((extent, KVH * HD), values.dtype), values], axis=0)
    id_pad = jnp.concatenate([jnp.full((extent,), -1, jnp.int32), doc_ids.astype(jnp.int32)], axis=0)
    lagged = jnp.arange(window, dtype=jnp.int32)[None, :] - extent
    ahead = jnp.arange(TOK_DEV, dtype=jnp.int32)[:, None]
    causal = lagged <= ahead

    def one_block(block_index):
        start = (block_index * TOK_DEV).astype(jnp.int32)
        query_block = lax.dynamic_slice_in_dim(queries, start, TOK_DEV, 0).astype(jnp.float32).reshape(TOK_DEV, KVH, groups, HD)
        key_block = lax.dynamic_slice_in_dim(key_pad, start, window, 0).astype(jnp.float32).reshape(window, KVH, HD)
        value_block = lax.dynamic_slice_in_dim(value_pad, start, window, 0).astype(jnp.float32).reshape(window, KVH, HD)
        query_ids = lax.dynamic_slice_in_dim(doc_ids.astype(jnp.int32), start, TOK_DEV, 0)
        key_ids = lax.dynamic_slice_in_dim(id_pad, start, window, 0)
        visible = (query_ids[:, None] == key_ids[None, :]) & causal
        scores = jnp.einsum("qcgd,kcd->qcgk", query_block, key_block, precision=lax.Precision.HIGHEST) * scaling
        scores = jnp.where(visible[:, None, None, :], scores, -jnp.inf)
        peak = jnp.max(scores, axis=-1, keepdims=True)
        weights = jnp.exp(scores - peak)
        total = jnp.sum(weights, axis=-1)
        rounded = lax.optimization_barrier(weights.astype(jnp.bfloat16))
        numerator = jnp.einsum("qcgk,kcd->qcgd", rounded.astype(jnp.float32), value_block, precision=lax.Precision.HIGHEST)
        return (numerator / total[..., None]).reshape(TOK_DEV, QH * HD).astype(jnp.bfloat16)

    blocks = lax.map(one_block, jnp.arange(TOKENS // TOK_DEV, dtype=jnp.int32))
    return blocks.reshape(TOKENS, QH * HD)
```

```python
import functools

import jax
import jax.numpy as jnp
from jax import lax
from jax.experimental import pallas as pl
from jax.experimental.pallas import tpu as pltpu
from jax.sharding import PartitionSpec as P

QH = 64
KVH = 8
HD = 128
REACH = 7
GROUPS = QH // KVH
MESH = pl.DeviceIdType.MESH
NEG = -1e30
LOWEST = -3e38
SCALE = HD ** -0.5 * 1.4426950408889634


def kernel(
    tok_len, head_len, hops,
    q_hbm, k_hbm, v_hbm, ids_ref, out_ref,
    q_buf, kv, bias, peak, part, acc,
    own_sem, q_own_sem, mate_send, mate_recv, far_send, far_recv, q_send, q_recv,
    raw_z_send, raw_x_send, z_send, z_recv, x_send, x_recv, lift_send, lift_recv,
):
    t, h = lax.axis_index("tok"), lax.axis_index("head")
    level, parity = t // 2, lax.rem(t, 2)
    pair, member = h // 2, lax.rem(h, 2)
    other = 1 - parity
    partner, mate = level * 2 + other, pair * 2 + (1 - member)
    levels, pairs = tok_len // 2, head_len // 2
    piece = q_hbm.shape[0]
    kv_heads, shard, wide = q_buf.shape
    q_cols, kv_cols = kv_heads * wide, kv_heads * HD
    unit_keys = 2 * piece
    lanes = part.shape[2]
    sources = (k_hbm, v_hbm)
    up, down = level + 1 < levels, level >= 1

    def by_parity(rule):
        return parity * int(rule(1)) + (1 - parity) * int(rule(0)) == 1

    def climbs(k, p):
        return k <= hops and (2 * k <= REACH or 2 * k + 1 - 2 * p <= REACH)

    def crosses(k, p):
        return k <= hops and 0 <= 2 * k + 1 - 2 * p <= REACH

    def column(start, size):
        return pl.ds(pl.multiple_of(start, size), size)

    def unit(k, s, d):
        return kv.at[2 * k + s, lax.rem(pair + d, pairs)]

    def remote(src, dst, send, recv, tok, head):
        return pltpu.make_async_remote_copy(
            src_ref=src, dst_ref=dst, send_sem=send, recv_sem=recv,
            device_id={"tok": tok, "head": head}, device_id_type=MESH,
        )

    def raw(g, which):
        return sources[which].at[:, column(g * kv_cols, kv_cols)]

    def place(k, s, which):
        return kv.at[2 * k + s, pair, 2 * member + which]

    def raw_z(i, which):
        g = (h, mate)[i]
        return remote(raw(g, which), place(1, parity, which), raw_z_send.at[i, which], z_recv.at[1, 0], t + 2, g)

    def raw_x(i, which):
        g = (h, mate)[i]
        return remote(raw(g, which), place(0, 0, which), raw_x_send.at[i, which], x_recv.at[0, 0], partner, g)

    def raw_mate(which):
        return remote(raw(mate, which), place(0, parity, which), mate_send.at[which], mate_recv.at[which], t, mate)

    def raw_own(which):
        return pltpu.make_async_copy(raw(h, which), place(0, parity, which), own_sem.at[which])

    def raw_far(d, m, which):
        g = lax.rem(pair + d, pairs) * 2 + m
        return remote(raw(g, which), place(0, parity, which), far_send.at[d, m, which], far_recv.at[pairs - d], t, g)

    def q_rows(hh, c):
        return q_buf.at[c, pl.ds(pl.multiple_of(hh * piece, piece), piece), :]

    def q_cols_of(g, c):
        return q_hbm.at[:, column(g * q_cols + c * wide, wide)]

    def q_far(d, m, c):
        g = lax.rem(pair + d, pairs) * 2 + m
        return remote(q_cols_of(g, c), q_rows(h, c), q_send.at[d, m, c], q_recv.at[pairs - d, c], t, g)

    def q_mate(c):
        return remote(q_cols_of(mate, c), q_rows(h, c), q_send.at[0, 0, c], q_recv.at[0, c], t, mate)

    def q_own(c):
        return pltpu.make_async_copy(q_cols_of(h, c), q_rows(h, c), q_own_sem.at[c])

    def push(k, d):
        return remote(unit(k, parity, d), unit(k + 1, parity, d), z_send.at[k + 1, d], z_recv.at[k + 1, d], t + 2, h)

    def share(k, d):
        return remote(unit(k, parity, d), unit(k, parity, d), x_send.at[k, d], x_recv.at[k, d], partner, h)

    def lift(d):
        return remote(unit(0, 0, d), unit(1, 0, d), lift_send.at[d], lift_recv.at[d], t + 2, h)

    barrier = pltpu.get_barrier_semaphore()

    def greet(tok, head):
        pl.semaphore_signal(barrier, inc=1, device_id={"tok": tok, "head": head}, device_id_type=MESH)

    for d in range(1, head_len):
        greet(t, lax.rem(h + d, head_len))
    for g in (h, mate):
        greet(partner, g)

        @pl.when(up)
        def _():
            greet(t + 2, g)

        @pl.when(down)
        def _():
            greet(t - 2, g)
    pl.semaphore_wait(
        barrier, head_len + 1 + 2 * jnp.minimum(levels - 1 - level, 1) + 2 * jnp.minimum(level, 1)
    )

    far = [(d, m) for d in range(1, pairs) for m in range(2)]
    for d, m in far:
        for which in range(2):
            raw_far(d, m, which).start()

    @pl.when(up)
    def _():
        for i in range(2):
            for which in range(2):
                raw_z(i, which).start()

    @pl.when(parity == 0)
    def _():
        for i in range(2):
            for which in range(2):
                raw_x(i, which).start()
    for which in range(2):
        raw_mate(which).start()
        raw_own(which).start()
    for c in range(kv_heads):
        q_mate(c).start()
        q_own(c).start()
    for c in range(kv_heads):
        for d, m in far:
            q_far(d, m, c).start()

    own_ids = ids_ref[:, column(t * shard, shard)]
    id_column = jnp.broadcast_to(own_ids, (shard, shard)).T
    q_pos = t * shard + lax.broadcasted_iota(jnp.int32, (shard, shard), 0)
    k_iota = lax.broadcasted_iota(jnp.int32, (shard, shard), 1)
    for k in range(hops + 1):
        @pl.when(level >= k)
        def _():
            for s in range(2):
                start = ((level - k) * 2 + s) * shard
                key_ids = ids_ref[:, column(start, shard)]
                visible = (id_column == key_ids) & (start + k_iota <= q_pos)
                shown = jnp.where(visible, 0.0, NEG)
                for p in range(pairs):
                    bias[2 * k + s, p] = shown[:, p * unit_keys:(p + 1) * unit_keys]

    def clear(i, carry):
        peak[i] = jnp.full((shard, HD), LOWEST, jnp.float32)
        part[i] = jnp.zeros((shard, lanes), jnp.float32)
        acc[i] = jnp.zeros((shard, HD), jnp.float32)
        return carry

    lax.fori_loop(0, kv_heads * GROUPS, clear, 0)

    def absorb(row, size, c, units):
        heads = pl.ds(pl.multiple_of(c * HD, HD), HD)
        rows = pl.ds(pl.multiple_of(row, piece), size)
        spots = [(2 * k + s, lax.rem(pair + d, pairs)) for k, s, d in units]

        def gather(which):
            return jnp.concatenate([kv[a, b, 2 * m + which, :, heads] for a, b in spots for m in range(2)], axis=0)

        q = jnp.concatenate([q_buf[c, rows, i * HD:(i + 1) * HD] for i in range(GROUPS)], axis=0)
        scores = lax.dot_general(
            q, gather(0), (((1,), (1,)), ((), ())), preferred_element_type=jnp.float32
        )
        rounded, decays = [], []
        for i in range(GROUPS):
            index = c * GROUPS + i
            tiles = []
            for n, (a, b) in enumerate(spots):
                mine = scores[i * size:(i + 1) * size, n * unit_keys:(n + 1) * unit_keys]
                mine = mine * SCALE + bias[a, b, rows, :]
                tiles += [mine[:, x:x + lanes] for x in range(0, unit_keys, lanes)]
            top = functools.reduce(jnp.maximum, tiles)
            top = jnp.broadcast_to(jnp.max(top, axis=1, keepdims=True), (size, HD))
            before = peak[index, rows, :]
            top = jnp.maximum(before, top)
            decay = jnp.exp2(before - top)
            decays.append(decay)
            peak[index, rows, :] = top
            weights = [jnp.exp2(tile - top[:, :lanes]) for tile in tiles]
            part[index, rows, :] = part[index, rows, :] * decay[:, :lanes] + functools.reduce(jnp.add, weights)
            rounded.append(jnp.concatenate([w.astype(jnp.bfloat16) for w in weights], axis=1))
        update = jnp.dot(jnp.concatenate(rounded, axis=0), gather(1), preferred_element_type=jnp.float32)
        for i in range(GROUPS):
            index = c * GROUPS + i
            acc[index, rows, :] = acc[index, rows, :] * decays[i] + update[i * size:(i + 1) * size]

    def near_rows(units):
        def run(c, carry):
            absorb(pair * unit_keys, unit_keys, c, units)
            return carry

        lax.fori_loop(0, kv_heads, run, 0)

    def far_rows(c, units):
        def run(d, carry):
            absorb(lax.rem(pair + d, pairs) * unit_keys, unit_keys, c, units)
            return carry

        lax.fori_loop(1, pairs, run, 0)

    def all_rows(units, between=None):
        if between is None:
            def run(c, carry):
                absorb(0, shard, c, units)
                return carry

            lax.fori_loop(0, kv_heads, run, 0)
        else:
            absorb(0, shard, 0, units)
            between()
            for c in range(1, kv_heads):
                absorb(0, shard, c, units)

    whole, near_only, far_only = range(pairs), range(1), range(1, pairs)

    def of(k, s, ds):
        return [(k, s, d) for d in ds]

    def first(rows):
        rows(of(0, parity, whole))

    def second(rows):
        @pl.when((parity == 1) & down)
        def _():
            rows(of(0, other, whole) + of(1, parity, whole))

        @pl.when((parity == 1) & (level == 0))
        def _():
            rows(of(0, other, whole))

        @pl.when((parity == 0) & down)
        def _():
            rows(of(1, parity, whole))

    def third(rows):
        if hops >= 2:
            @pl.when(level >= 2)
            def _():
                rows(of(1, other, whole) + of(2, parity, near_only) + of(2, other, near_only))

        @pl.when((level == 1) if hops >= 2 else down)
        def _():
            rows(of(1, other, whole))

    def climbed(k, ds):
        if k > hops:
            return

        @pl.when((level >= k) & by_parity(lambda p: climbs(k, p)))
        def _():
            for d in ds:
                push(k - 1, d).wait_recv()

                @pl.when(up & by_parity(lambda p: climbs(k + 1, p)))
                def _():
                    push(k, d).start()

                @pl.when(by_parity(lambda p: crosses(k, p) and not (k == 1 and d >= 1 and p == 0)))
                def _():
                    share(k, d).start()

    def crossed(k, ds):
        if k > hops:
            return
        for d in ds:
            @pl.when((level >= k) & by_parity(lambda p: crosses(k, 1 - p) and not (k == 1 and d >= 1 and p == 1)))
            def _():
                share(k, d).wait_recv()
                if k == 0 and d >= 1:
                    @pl.when(up)
                    def _():
                        lift(d).start()

            if k == 1 and d >= 1:
                @pl.when(down & (parity == 1))
                def _():
                    lift(d).wait_recv()

    for which in range(2):
        raw_own(which).wait()
        raw_mate(which).wait_recv()
    for d in far_only:
        push_d = unit(0, parity, d)
        remote(push_d, push_d, far_send.at[d, 0, 0], far_recv.at[d], t, mate).wait_recv()

        @pl.when(up)
        def _():
            push(0, d).start()

        @pl.when(parity == 0)
        def _():
            share(0, d).start()
    climbed(1, near_only)
    for c in range(kv_heads):
        q_own(c).wait()
        q_mate(c).wait_recv()
    near_rows(of(0, parity, whole))
    climbed(1, far_only)
    crossed(0, whole)
    second(near_rows)
    climbed(2, near_only)

    def await_q(c):
        for d in far_only:
            block = q_buf.at[c, column(lax.rem(pair + d, pairs) * unit_keys, unit_keys), :]
            remote(block, block, q_send.at[d, 0, c], q_recv.at[d, c], t, mate).wait_recv()

    await_q(0)
    far_rows(0, of(0, parity, whole))
    second(functools.partial(far_rows, 0))
    climbed(2, far_only)
    crossed(1, whole)
    crossed(2, near_only)
    third(near_rows)
    climbed(3, near_only)
    third(functools.partial(far_rows, 0))
    for c in range(1, kv_heads):
        await_q(c)
        far_rows(c, of(0, parity, whole))
        second(functools.partial(far_rows, c))
        third(functools.partial(far_rows, c))
    crossed(2, far_only)
    if hops >= 2:
        @pl.when(level >= 2)
        def _():
            all_rows(of(2, parity, far_only) + of(2, other, far_only))
    climbed(3, far_only)
    climbed(4, whole)
    crossed(3, near_only)
    if hops >= 3:
        @pl.when(level >= 3)
        def _():
            all_rows(of(3, parity, near_only) + of(3, other, near_only))
    crossed(3, far_only)
    if hops >= 3:
        @pl.when(level >= 3)
        def _():
            all_rows(of(3, parity, far_only) + of(3, other, far_only))
    crossed(4, whole)
    if hops >= 4:
        @pl.when((level >= 4) & (parity == 0))
        def _():
            all_rows(of(4, 1, whole))

    def finish(index, carry):
        total = jnp.sum(part[index], axis=1, keepdims=True)
        result = (acc[index] * (1.0 / total)).astype(out_ref.dtype)
        out_ref[:, pl.ds(pl.multiple_of(index * HD, HD), HD)] = result
        return carry

    lax.fori_loop(0, kv_heads * GROUPS, finish, 0, unroll=2)

    for d, m in far:
        for which in range(2):
            raw_far(d, m, which).wait_send()
        for c in range(kv_heads):
            q_far(d, m, c).wait_send()
    for which in range(2):
        raw_mate(which).wait_send()
    for c in range(kv_heads):
        q_mate(c).wait_send()

    @pl.when(up)
    def _():
        for i in range(2):
            for which in range(2):
                raw_z(i, which).wait_send()
        for d in far_only:
            push(0, d).wait_send()

    @pl.when(parity == 0)
    def _():
        for i in range(2):
            for which in range(2):
                raw_x(i, which).wait_send()
        for d in far_only:
            share(0, d).wait_send()

    @pl.when(up & (parity == 1))
    def _():
        for d in far_only:
            lift(d).wait_send()
    for k in range(1, hops + 1):
        @pl.when((level >= k) & by_parity(lambda p: climbs(k, p)))
        def _():
            for d in whole:
                @pl.when(up & by_parity(lambda p: climbs(k + 1, p)))
                def _():
                    push(k, d).wait_send()

                @pl.when(by_parity(lambda p: crosses(k, p) and not (k == 1 and d >= 1 and p == 0)))
                def _():
                    share(k, d).wait_send()


def body(queries, keys, values, doc_ids):
    tok_len, head_len = lax.axis_size("tok"), lax.axis_size("head")
    piece = queries.shape[0]
    shard = piece * head_len
    kv_heads = KVH // head_len
    pairs = head_len // 2
    wide = GROUPS * HD
    hops = min((REACH + 1) // 2, tok_len // 2 - 1)
    heads = kv_heads * GROUPS
    lanes = min(HD, 2 * piece)
    DMA = pltpu.SemaphoreType.DMA
    anywhere = pl.BlockSpec(memory_space=pl.ANY)
    vmem = pl.BlockSpec(memory_space=pltpu.VMEM)
    return pl.pallas_call(
        functools.partial(kernel, tok_len, head_len, hops),
        out_shape=jax.ShapeDtypeStruct((shard, heads * HD), jnp.bfloat16),
        in_specs=[anywhere, anywhere, anywhere, vmem],
        out_specs=vmem,
        scratch_shapes=[
            pltpu.VMEM((kv_heads, shard, wide), jnp.bfloat16),
            pltpu.VMEM((2 * (hops + 1), pairs, 4, piece, kv_heads * HD), jnp.bfloat16),
            pltpu.VMEM((2 * (hops + 1), pairs, shard, 2 * piece), jnp.float32),
            pltpu.VMEM((heads, shard, HD), jnp.float32),
            pltpu.VMEM((heads, shard, lanes), jnp.float32),
            pltpu.VMEM((heads, shard, HD), jnp.float32),
            DMA((2,)),
            DMA((kv_heads,)),
            DMA((2,)),
            DMA((2,)),
            DMA((pairs, 2, 2)),
            DMA((pairs,)),
            DMA((pairs, 2, kv_heads)),
            DMA((pairs, kv_heads)),
            DMA((2, 2)),
            DMA((2, 2)),
            DMA((hops + 2, pairs)),
            DMA((hops + 2, pairs)),
            DMA((hops + 1, pairs)),
            DMA((hops + 1, pairs)),
            DMA((pairs,)),
            DMA((pairs,)),
        ],
        compiler_params=pltpu.CompilerParams(
            collective_id=0, has_side_effects=True, vmem_limit_bytes=60 * 1000 * 1000
        ),
    )(queries, keys, values, doc_ids.reshape(1, -1))


def solution(mesh):
    return jax.shard_map(
        body,
        mesh=mesh,
        in_specs=(
            P(("tok", "head"), None),
            P(("tok", "head"), None),
            P(("tok", "head"), None),
            P(),
        ),
        out_specs=P("tok", "head"),
        check_vma=False,
    )
```

```python
import functools

import jax
import jax.numpy as jnp
from jax import lax
from jax.experimental import pallas as pl
from jax.experimental.pallas import tpu as pltpu
from jax.sharding import PartitionSpec as P

QH = 64
KVH = 8
HD = 128
REACH = 7
GROUPS = QH // KVH
MESH = pl.DeviceIdType.MESH
NEG = -1e30
LOWEST = -3e38
SCALE = HD ** -0.5 * 1.4426950408889634


def kernel(
    tok_len, head_len, hops,
    q_hbm, k_hbm, v_hbm, ids_hbm, out_ref,
    ids_ref, q_buf, kv, bias, peak, part, acc,
    own_sem, q_own_sem, mate_send, mate_recv, far_send, far_recv, q_send, q_recv,
    raw_z_send, raw_x_send, z_send, z_recv, x_send, x_recv, lift_send, lift_recv, ids_sem, ready,
):
    t, h = lax.axis_index("tok"), lax.axis_index("head")
    level, parity = t // 2, lax.rem(t, 2)
    pair, member = h // 2, lax.rem(h, 2)
    other = 1 - parity
    partner, mate = level * 2 + other, pair * 2 + (1 - member)
    levels, pairs = tok_len // 2, head_len // 2
    piece = q_hbm.shape[0]
    kv_heads, shard, wide = q_buf.shape
    q_cols, kv_cols = kv_heads * wide, kv_heads * HD
    unit_keys = 2 * piece
    lanes = part.shape[2]
    sources = (k_hbm, v_hbm)
    up, down = level + 1 < levels, level >= 1

    def by_parity(rule):
        return parity * int(rule(1)) + (1 - parity) * int(rule(0)) == 1

    def climbs(k, p):
        return k <= hops and (2 * k <= REACH or 2 * k + 1 - 2 * p <= REACH)

    def crosses(k, p):
        return k <= hops and 0 <= 2 * k + 1 - 2 * p <= REACH

    def column(start, size):
        return pl.ds(pl.multiple_of(start, size), size)

    def half(k, s, d, m):
        return kv.at[2 * k + s, lax.rem(pair + d, pairs), 2 * m:2 * m + 2]

    def remote(src, dst, send, recv, tok, head):
        return pltpu.make_async_remote_copy(
            src_ref=src, dst_ref=dst, send_sem=send, recv_sem=recv,
            device_id={"tok": tok, "head": head}, device_id_type=MESH,
        )

    def raw(g, which):
        return sources[which].at[:, column(g * kv_cols, kv_cols)]

    def place(k, s, which):
        return kv.at[2 * k + s, pair, 2 * member + which]

    def raw_z(i, which):
        g = (h, mate)[i]
        return remote(raw(g, which), place(1, parity, which), raw_z_send.at[i, which], z_recv.at[1, 0, member], t + 2, g)

    def raw_x(i, which):
        g = (h, mate)[i]
        return remote(raw(g, which), place(0, 0, which), raw_x_send.at[i, which], x_recv.at[0, 0, member], partner, g)

    def raw_mate(which):
        return remote(raw(mate, which), place(0, parity, which), mate_send.at[which], mate_recv.at[which], t, mate)

    def raw_own(which):
        return pltpu.make_async_copy(raw(h, which), place(0, parity, which), own_sem.at[which])

    def raw_far(d, m, which):
        g = lax.rem(pair + d, pairs) * 2 + m
        return remote(raw(g, which), place(0, parity, which), far_send.at[d, m, which], far_recv.at[pairs - d, member], t, g)

    def q_rows(hh, c):
        return q_buf.at[c, pl.ds(pl.multiple_of(hh * piece, piece), piece), :]

    def q_cols_of(g, c):
        return q_hbm.at[:, column(g * q_cols + c * wide, wide)]

    def q_far(d, m, c):
        g = lax.rem(pair + d, pairs) * 2 + m
        return remote(q_cols_of(g, c), q_rows(h, c), q_send.at[d, m, c], q_recv.at[pairs - d, c], t, g)

    def q_mate(c):
        return remote(q_cols_of(mate, c), q_rows(h, c), q_send.at[0, 0, c], q_recv.at[0, c], t, mate)

    def q_own(c):
        return pltpu.make_async_copy(q_cols_of(h, c), q_rows(h, c), q_own_sem.at[c])

    def push(k, d, m):
        return remote(
            half(k, parity, d, m), half(k + 1, parity, d, m), z_send.at[k + 1, d, m], z_recv.at[k + 1, d, m], t + 2, h
        )

    def share(k, d, m):
        return remote(half(k, parity, d, m), half(k, parity, d, m), x_send.at[k, d, m], x_recv.at[k, d, m], partner, h)

    def lift(d, m):
        return remote(half(0, 0, d, m), half(1, 0, d, m), lift_send.at[d, m], lift_recv.at[d, m], t + 2, h)

    ids_copy = pltpu.make_async_copy(ids_hbm, ids_ref, ids_sem)
    ids_copy.start()
    for which in range(2):
        raw_own(which).start()
    for c in range(kv_heads):
        q_own(c).start()

    barrier = pltpu.get_barrier_semaphore()

    def greet(tok, head):
        pl.semaphore_signal(barrier, inc=1, device_id={"tok": tok, "head": head}, device_id_type=MESH)

    for d in range(1, head_len):
        greet(t, lax.rem(h + d, head_len))
    for g in (h, mate):
        greet(partner, g)

        @pl.when(up)
        def _():
            greet(t + 2, g)

    pl.semaphore_wait(barrier, head_len + 1 + 2 * jnp.minimum(level, 1))

    @pl.when(down)
    def _():
        for g in (h, mate):
            pl.semaphore_signal(ready, inc=1, device_id={"tok": t - 2, "head": g}, device_id_type=MESH)

    far = [(d, m) for d in range(1, pairs) for m in range(2)]
    for d, m in far:
        for which in range(2):
            raw_far(d, m, which).start()

    @pl.when(parity == 0)
    def _():
        for i in range(2):
            for which in range(2):
                raw_x(i, which).start()
    for which in range(2):
        raw_mate(which).start()
    for c in range(kv_heads):
        q_mate(c).start()
    for c in range(kv_heads):
        for d, m in far:
            q_far(d, m, c).start()

    @pl.when(up)
    def _():
        pl.semaphore_wait(ready, 2)
        for i in range(2):
            for which in range(2):
                raw_z(i, which).start()

    ids_copy.wait()

    own_ids = ids_ref[:, column(t * shard, shard)]
    id_column = jnp.broadcast_to(own_ids, (shard, shard)).T
    q_pos = t * shard + lax.broadcasted_iota(jnp.int32, (shard, shard), 0)
    k_iota = lax.broadcasted_iota(jnp.int32, (shard, shard), 1)
    for k in range(hops + 1):
        @pl.when(level >= k)
        def _():
            for s in range(2):
                start = ((level - k) * 2 + s) * shard
                key_ids = ids_ref[:, column(start, shard)]
                visible = (id_column == key_ids) & (start + k_iota <= q_pos)
                shown = jnp.where(visible, 0.0, NEG)
                for p in range(pairs):
                    bias[2 * k + s, p] = shown[:, p * unit_keys:(p + 1) * unit_keys]

    def clear(i, carry):
        peak[i] = jnp.full((shard, HD), LOWEST, jnp.float32)
        part[i] = jnp.zeros((shard, lanes), jnp.float32)
        acc[i] = jnp.zeros((shard, HD), jnp.float32)
        return carry

    lax.fori_loop(0, kv_heads * GROUPS, clear, 0)

    def absorb(row, size, c, units, final=False):
        heads = pl.ds(pl.multiple_of(c * HD, HD), HD)
        rows = pl.ds(pl.multiple_of(row, piece), size)
        spots = [(2 * k + s, lax.rem(pair + d, pairs)) for k, s, d in units]

        def gather(which):
            return jnp.concatenate([kv[a, b, 2 * m + which, :, heads] for a, b in spots for m in range(2)], axis=0)

        q = jnp.concatenate([q_buf[c, rows, i * HD:(i + 1) * HD] for i in range(GROUPS)], axis=0)
        scores = lax.dot_general(
            q, gather(0), (((1,), (1,)), ((), ())), preferred_element_type=jnp.float32
        )
        rounded, decays, totals = [], [], []
        for i in range(GROUPS):
            index = c * GROUPS + i
            tiles = []
            for n, (a, b) in enumerate(spots):
                mine = scores[i * size:(i + 1) * size, n * unit_keys:(n + 1) * unit_keys]
                mine = mine * SCALE + bias[a, b, rows, :]
                tiles += [mine[:, x:x + lanes] for x in range(0, unit_keys, lanes)]
            top = functools.reduce(jnp.maximum, tiles)
            top = jnp.broadcast_to(jnp.max(top, axis=1, keepdims=True), (size, HD))
            before = peak[index, rows, :]
            top = jnp.maximum(before, top)
            decay = jnp.exp2(before - top)
            decays.append(decay)
            weights = [jnp.exp2(tile - top[:, :lanes]) for tile in tiles]
            total = part[index, rows, :] * decay[:, :lanes] + functools.reduce(jnp.add, weights)
            if final:
                totals.append(1.0 / jnp.sum(total, axis=1, keepdims=True))
            else:
                peak[index, rows, :] = top
                part[index, rows, :] = total
            rounded.append(jnp.concatenate([w.astype(jnp.bfloat16) for w in weights], axis=1))
        update = jnp.dot(jnp.concatenate(rounded, axis=0), gather(1), preferred_element_type=jnp.float32)
        for i in range(GROUPS):
            index = c * GROUPS + i
            mine = acc[index, rows, :] * decays[i] + update[i * size:(i + 1) * size]
            if final:
                out_ref[rows, column(index * HD, HD)] = (mine * totals[i]).astype(out_ref.dtype)
            else:
                acc[index, rows, :] = mine

    def near_rows(units):
        def run(c, carry):
            absorb(pair * unit_keys, unit_keys, c, units)
            return carry

        lax.fori_loop(0, kv_heads, run, 0)

    def far_rows(c, units):
        def run(d, carry):
            absorb(lax.rem(pair + d, pairs) * unit_keys, unit_keys, c, units)
            return carry

        lax.fori_loop(1, pairs, run, 0)

    def all_rows(units, final=False):
        def run(c, carry):
            absorb(0, shard, c, units, final)
            return carry

        lax.fori_loop(0, kv_heads, run, 0)

    whole, near_only, far_only = range(pairs), range(1), range(1, pairs)

    def of(k, s, ds):
        return [(k, s, d) for d in ds]

    def first(rows):
        rows(of(0, parity, whole))

    def second(rows):
        @pl.when((parity == 1) & down)
        def _():
            rows(of(0, other, whole) + of(1, parity, whole))

        @pl.when((parity == 1) & (level == 0))
        def _():
            rows(of(0, other, whole))

        @pl.when((parity == 0) & down)
        def _():
            rows(of(1, parity, whole))

    def deeper(rows, units):
        if hops >= 2:
            @pl.when(level >= 2)
            def _():
                rows(units)

    def third(rows):
        deeper(rows, of(1, other, near_only) + of(2, parity, near_only))

        @pl.when((level == 1) if hops >= 2 else down)
        def _():
            rows(of(1, other, near_only))

    def fourth(rows):
        deeper(rows, of(2, parity, far_only) + of(2, other, near_only))

    def third_and_fourth(rows):
        deeper(rows, of(1, other, near_only) + of(2, parity, whole) + of(2, other, near_only))

        @pl.when((level == 1) if hops >= 2 else down)
        def _():
            rows(of(1, other, near_only))

    def climbed(k, ds):
        if k > hops:
            return

        @pl.when((level >= k) & by_parity(lambda p: climbs(k, p)))
        def _():
            for d in ds:
                for m in range(2):
                    push(k - 1, d, m).wait_recv()

                    @pl.when(up & by_parity(lambda p: climbs(k + 1, p)))
                    def _():
                        push(k, d, m).start()

                    @pl.when(by_parity(lambda p: crosses(k, p) and not (k == 1 and d >= 1 and p == 0)))
                    def _():
                        share(k, d, m).start()

    def crossed(k, ds):
        if k > hops:
            return
        for d in ds:
            @pl.when((level >= k) & by_parity(lambda p: crosses(k, 1 - p) and not (k == 1 and d >= 1 and p == 1)))
            def _():
                for m in range(2):
                    share(k, d, m).wait_recv()

            if k == 1 and d >= 1:
                @pl.when(down & (parity == 1))
                def _():
                    for m in range(2):
                        lift(d, m).wait_recv()

    for which in range(2):
        raw_own(which).wait()
        raw_mate(which).wait_recv()
    for d in far_only:
        for m in range(2):
            mine = half(0, parity, d, m)
            remote(mine, mine, far_send.at[d, 0, 0], far_recv.at[d, m], t, mate).wait_recv()

            @pl.when(up)
            def _():
                push(0, d, m).start()

            @pl.when(parity == 0)
            def _():
                share(0, d, m).start()
    climbed(1, near_only)
    for c in range(kv_heads):
        q_own(c).wait()
        q_mate(c).wait_recv()
    near_rows(of(0, parity, whole))
    climbed(1, far_only)
    crossed(0, whole)
    second(near_rows)
    climbed(2, near_only)

    def await_q(c):
        for d in far_only:
            block = q_buf.at[c, column(lax.rem(pair + d, pairs) * unit_keys, unit_keys), :]
            remote(block, block, q_send.at[d, 0, c], q_recv.at[d, c], t, mate).wait_recv()

    await_q(0)
    far_rows(0, of(0, parity, whole))
    second(functools.partial(far_rows, 0))
    crossed(1, near_only)
    third(near_rows)
    third(functools.partial(far_rows, 0))
    climbed(2, far_only)

    @pl.when(up & (parity == 1))
    def _():
        for d in far_only:
            for m in range(2):
                lift(d, m).start()

    crossed(2, near_only)
    fourth(near_rows)
    fourth(functools.partial(far_rows, 0))
    climbed(3, near_only)
    for c in range(1, kv_heads):
        await_q(c)
        far_rows(c, of(0, parity, whole))
        second(functools.partial(far_rows, c))
        third_and_fourth(functools.partial(far_rows, c))
    crossed(2, far_only)
    for c in range(kv_heads):
        if hops >= 3:
            @pl.when(level >= 3)
            def _():
                absorb(0, shard, c, of(2, other, far_only) + of(3, parity, near_only))
        if c == 0:
            climbed(3, far_only)
    climbed(4, whole)
    crossed(3, near_only)
    if hops >= 3:
        @pl.when(level >= 3)
        def _():
            all_rows(of(3, parity, far_only) + of(3, other, near_only))
    crossed(1, far_only)
    crossed(3, far_only)
    fused = hops == 3
    if hops >= 3:
        @pl.when(level >= 3)
        def _():
            all_rows(of(1, other, far_only) + of(3, other, far_only), final=fused)
    if hops >= 2:
        @pl.when((level == 2) if hops >= 3 else (level >= 2))
        def _():
            all_rows(of(2, other, far_only) + of(1, other, far_only))

    @pl.when((level == 1) if hops >= 2 else down)
    def _():
        all_rows(of(1, other, far_only))
    crossed(4, whole)
    if hops >= 4:
        @pl.when((level >= 4) & (parity == 0))
        def _():
            all_rows(of(4, 1, whole))

    def finish(index, carry):
        total = jnp.sum(part[index], axis=1, keepdims=True)
        result = (acc[index] * (1.0 / total)).astype(out_ref.dtype)
        out_ref[:, pl.ds(pl.multiple_of(index * HD, HD), HD)] = result
        return carry

    @pl.when(level < (3 if fused else levels))
    def _():
        lax.fori_loop(0, kv_heads * GROUPS, finish, 0, unroll=2)

    for d, m in far:
        for which in range(2):
            raw_far(d, m, which).wait_send()
        for c in range(kv_heads):
            q_far(d, m, c).wait_send()
    for which in range(2):
        raw_mate(which).wait_send()
    for c in range(kv_heads):
        q_mate(c).wait_send()

    @pl.when(up)
    def _():
        for i in range(2):
            for which in range(2):
                raw_z(i, which).wait_send()
        for d in far_only:
            for m in range(2):
                push(0, d, m).wait_send()

    @pl.when(parity == 0)
    def _():
        for i in range(2):
            for which in range(2):
                raw_x(i, which).wait_send()
        for d in far_only:
            for m in range(2):
                share(0, d, m).wait_send()

    @pl.when(up & (parity == 1))
    def _():
        for d in far_only:
            for m in range(2):
                lift(d, m).wait_send()
    for k in range(1, hops + 1):
        @pl.when((level >= k) & by_parity(lambda p: climbs(k, p)))
        def _():
            for d in whole:
                for m in range(2):
                    @pl.when(up & by_parity(lambda p: climbs(k + 1, p)))
                    def _():
                        push(k, d, m).wait_send()

                    @pl.when(by_parity(lambda p: crosses(k, p) and not (k == 1 and d >= 1 and p == 0)))
                    def _():
                        share(k, d, m).wait_send()


def body(queries, keys, values, doc_ids):
    tok_len, head_len = lax.axis_size("tok"), lax.axis_size("head")
    piece = queries.shape[0]
    shard = piece * head_len
    kv_heads = KVH // head_len
    pairs = head_len // 2
    wide = GROUPS * HD
    hops = min((REACH + 1) // 2, tok_len // 2 - 1)
    heads = kv_heads * GROUPS
    lanes = min(HD, 2 * piece)
    DMA = pltpu.SemaphoreType.DMA
    anywhere = pl.BlockSpec(memory_space=pl.ANY)
    vmem = pl.BlockSpec(memory_space=pltpu.VMEM)
    return pl.pallas_call(
        functools.partial(kernel, tok_len, head_len, hops),
        out_shape=pltpu.VMEM((shard, heads * HD), jnp.bfloat16),
        in_specs=[anywhere] * 4,
        out_specs=vmem,
        scratch_shapes=[
            pltpu.VMEM((1, doc_ids.shape[0]), jnp.int32),
            pltpu.VMEM((kv_heads, shard, wide), jnp.bfloat16),
            pltpu.VMEM((2 * (hops + 1), pairs, 4, piece, kv_heads * HD), jnp.bfloat16),
            pltpu.VMEM((2 * (hops + 1), pairs, shard, 2 * piece), jnp.float32),
            pltpu.VMEM((heads, shard, HD), jnp.float32),
            pltpu.VMEM((heads, shard, lanes), jnp.float32),
            pltpu.VMEM((heads, shard, HD), jnp.float32),
            DMA((2,)),
            DMA((kv_heads,)),
            DMA((2,)),
            DMA((2,)),
            DMA((pairs, 2, 2)),
            DMA((pairs, 2)),
            DMA((pairs, 2, kv_heads)),
            DMA((pairs, kv_heads)),
            DMA((2, 2)),
            DMA((2, 2)),
            DMA((hops + 2, pairs, 2)),
            DMA((hops + 2, pairs, 2)),
            DMA((hops + 1, pairs, 2)),
            DMA((hops + 1, pairs, 2)),
            DMA((pairs, 2)),
            DMA((pairs, 2)),
            DMA,
            pltpu.SemaphoreType.REGULAR,
        ],
        compiler_params=pltpu.CompilerParams(
            collective_id=0, has_side_effects=True, vmem_limit_bytes=32 * 1000 * 1000
        ),
    )(*(pltpu.with_memory_space_constraint(a, pltpu.HBM) for a in (queries, keys, values, doc_ids.reshape(1, -1))))


def solution(mesh):
    return jax.shard_map(
        body,
        mesh=mesh,
        in_specs=(
            P(("tok", "head"), None),
            P(("tok", "head"), None),
            P(("tok", "head"), None),
            P(),
        ),
        out_specs=P("tok", "head"),
        check_vma=False,
    )
```

```python
import functools

import jax
import jax.numpy as jnp
from jax import lax
from jax.experimental import pallas as pl
from jax.experimental.pallas import tpu as pltpu
from jax.sharding import PartitionSpec as P

QH = 64
KVH = 8
HD = 128
REACH = 7
GROUPS = QH // KVH
MESH = pl.DeviceIdType.MESH
NEG = -1e30
LOWEST = -3e38
SCALE = HD ** -0.5 * 1.4426950408889634


def kernel(
    tok_len, head_len, hops,
    q_hbm, k_hbm, v_hbm, ids_hbm, out_ref,
    ids_ref, q_buf, kv, bias, peak, part, acc,
    own_sem, q_own_sem, mate_send, mate_recv, far_send, far_recv, q_send, q_recv,
    raw_z_send, raw_x_send, z_send, z_recv, x_send, x_recv, lift_send, lift_recv, ids_sem, ready,
):
    t, h = lax.axis_index("tok"), lax.axis_index("head")
    level, parity = t // 2, lax.rem(t, 2)
    pair, member = h // 2, lax.rem(h, 2)
    other = 1 - parity
    partner, mate = level * 2 + other, pair * 2 + (1 - member)
    levels, pairs = tok_len // 2, head_len // 2
    piece = q_hbm.shape[0]
    kv_heads, shard, wide = q_buf.shape
    q_cols, kv_cols = kv_heads * wide, kv_heads * HD
    unit_keys = 2 * piece
    lanes = part.shape[2]
    sources = (k_hbm, v_hbm)
    up, down = level + 1 < levels, level >= 1

    def by_parity(rule):
        return parity * int(rule(1)) + (1 - parity) * int(rule(0)) == 1

    def climbs(k, p):
        return k <= hops and (2 * k <= REACH or 2 * k + 1 - 2 * p <= REACH)

    def crosses(k, p):
        return k <= hops and 0 <= 2 * k + 1 - 2 * p <= REACH

    def column(start, size):
        return pl.ds(pl.multiple_of(start, size), size)

    def half(k, s, d, m):
        return kv.at[2 * k + s, lax.rem(pair + d, pairs), 2 * m:2 * m + 2]

    def remote(src, dst, send, recv, tok, head):
        return pltpu.make_async_remote_copy(
            src_ref=src, dst_ref=dst, send_sem=send, recv_sem=recv,
            device_id={"tok": tok, "head": head}, device_id_type=MESH,
        )

    def raw(g, which):
        return sources[which].at[:, column(g * kv_cols, kv_cols)]

    def place(k, s, which):
        return kv.at[2 * k + s, pair, 2 * member + which]

    def raw_z(i, which):
        g = (h, mate)[i]
        return remote(raw(g, which), place(1, parity, which), raw_z_send.at[i, which], z_recv.at[1, 0, member], t + 2, g)

    def raw_x(i, which):
        g = (h, mate)[i]
        return remote(raw(g, which), place(0, 0, which), raw_x_send.at[i, which], x_recv.at[0, 0, member], partner, g)

    def raw_mate(which):
        return remote(raw(mate, which), place(0, parity, which), mate_send.at[which], mate_recv.at[which], t, mate)

    def raw_own(which):
        return pltpu.make_async_copy(raw(h, which), place(0, parity, which), own_sem.at[which])

    def raw_far(d, m, which):
        g = lax.rem(pair + d, pairs) * 2 + m
        return remote(raw(g, which), place(0, parity, which), far_send.at[d, m, which], far_recv.at[pairs - d, member], t, g)

    def q_rows(hh, c):
        return q_buf.at[c, pl.ds(pl.multiple_of(hh * piece, piece), piece), :]

    def q_cols_of(g, c):
        return q_hbm.at[:, column(g * q_cols + c * wide, wide)]

    def q_far(d, m, c):
        g = lax.rem(pair + d, pairs) * 2 + m
        return remote(q_cols_of(g, c), q_rows(h, c), q_send.at[d, m, c], q_recv.at[pairs - d, c], t, g)

    def q_mate(c):
        return remote(q_cols_of(mate, c), q_rows(h, c), q_send.at[0, 0, c], q_recv.at[0, c], t, mate)

    def q_own(c):
        return pltpu.make_async_copy(q_cols_of(h, c), q_rows(h, c), q_own_sem.at[c])

    def push(k, d, m):
        return remote(
            half(k, parity, d, m), half(k + 1, parity, d, m), z_send.at[k + 1, d, m], z_recv.at[k + 1, d, m], t + 2, h
        )

    def share(k, d, m):
        return remote(half(k, parity, d, m), half(k, parity, d, m), x_send.at[k, d, m], x_recv.at[k, d, m], partner, h)

    def lift(d, m):
        return remote(half(0, 0, d, m), half(1, 0, d, m), lift_send.at[d, m], lift_recv.at[d, m], t + 2, h)

    ids_copy = pltpu.make_async_copy(ids_hbm, ids_ref, ids_sem)
    ids_copy.start()
    for which in range(2):
        raw_own(which).start()
    for c in range(kv_heads):
        q_own(c).start()

    barrier = pltpu.get_barrier_semaphore()

    def greet(tok, head):
        pl.semaphore_signal(barrier, inc=1, device_id={"tok": tok, "head": head}, device_id_type=MESH)

    for d in range(1, head_len):
        greet(t, lax.rem(h + d, head_len))
    for g in (h, mate):
        greet(partner, g)

        @pl.when(up)
        def _():
            greet(t + 2, g)

    pl.semaphore_wait(barrier, head_len + 1 + 2 * jnp.minimum(level, 1))

    @pl.when(down)
    def _():
        for g in (h, mate):
            pl.semaphore_signal(ready, inc=1, device_id={"tok": t - 2, "head": g}, device_id_type=MESH)

    far = [(d, m) for d in range(1, pairs) for m in range(2)]
    for d, m in far:
        for which in range(2):
            raw_far(d, m, which).start()

    @pl.when(parity == 0)
    def _():
        for i in range(2):
            for which in range(2):
                raw_x(i, which).start()
    for which in range(2):
        raw_mate(which).start()
    for c in range(kv_heads):
        q_mate(c).start()
    for c in range(kv_heads):
        for d, m in far:
            q_far(d, m, c).start()

    @pl.when(up)
    def _():
        pl.semaphore_wait(ready, 2)
        for i in range(2):
            for which in range(2):
                raw_z(i, which).start()

    ids_copy.wait()

    own_ids = ids_ref[:, column(t * shard, shard)]
    id_column = jnp.broadcast_to(own_ids, (shard, shard)).T
    q_pos = t * shard + lax.broadcasted_iota(jnp.int32, (shard, shard), 0)
    k_iota = lax.broadcasted_iota(jnp.int32, (shard, shard), 1)
    for k in range(hops + 1):
        @pl.when(level >= k)
        def _():
            for s in range(2):
                start = ((level - k) * 2 + s) * shard
                key_ids = ids_ref[:, column(start, shard)]
                visible = (id_column == key_ids) & (start + k_iota <= q_pos)
                shown = jnp.where(visible, 0.0, NEG)
                for p in range(pairs):
                    bias[2 * k + s, p] = shown[:, p * unit_keys:(p + 1) * unit_keys]

    def clear(i, carry):
        peak[i] = jnp.full((shard, HD), LOWEST, jnp.float32)
        part[i] = jnp.zeros((shard, lanes), jnp.float32)
        acc[i] = jnp.zeros((shard, HD), jnp.float32)
        return carry

    lax.fori_loop(0, kv_heads * GROUPS, clear, 0)

    def absorb(row, size, c, units, final=False):
        heads = pl.ds(pl.multiple_of(c * HD, HD), HD)
        rows = pl.ds(pl.multiple_of(row, piece), size)
        spots = [(2 * k + s, lax.rem(pair + d, pairs)) for k, s, d in units]

        def gather(which):
            return jnp.concatenate([kv[a, b, 2 * m + which, :, heads] for a, b in spots for m in range(2)], axis=0)

        q = jnp.concatenate([q_buf[c, rows, i * HD:(i + 1) * HD] for i in range(GROUPS)], axis=0)
        scores = lax.dot_general(
            q, gather(0), (((1,), (1,)), ((), ())), preferred_element_type=jnp.float32
        )
        rounded, decays, totals = [], [], []
        for i in range(GROUPS):
            index = c * GROUPS + i
            tiles = []
            for n, (a, b) in enumerate(spots):
                mine = scores[i * size:(i + 1) * size, n * unit_keys:(n + 1) * unit_keys]
                mine = mine * SCALE + bias[a, b, rows, :]
                tiles += [mine[:, x:x + lanes] for x in range(0, unit_keys, lanes)]
            top = functools.reduce(jnp.maximum, tiles)
            top = jnp.broadcast_to(jnp.max(top, axis=1, keepdims=True), (size, HD))
            before = peak[index, rows, :]
            top = jnp.maximum(before, top)
            decay = jnp.exp2(before - top)
            decays.append(decay)
            weights = [jnp.exp2(tile - top[:, :lanes]) for tile in tiles]
            total = part[index, rows, :] * decay[:, :lanes] + functools.reduce(jnp.add, weights)
            if final:
                totals.append(1.0 / jnp.sum(total, axis=1, keepdims=True))
            else:
                peak[index, rows, :] = top
                part[index, rows, :] = total
            rounded.append(jnp.concatenate([w.astype(jnp.bfloat16) for w in weights], axis=1))
        update = jnp.dot(jnp.concatenate(rounded, axis=0), gather(1), preferred_element_type=jnp.float32)
        for i in range(GROUPS):
            index = c * GROUPS + i
            mine = acc[index, rows, :] * decays[i] + update[i * size:(i + 1) * size]
            if final:
                out_ref[rows, column(index * HD, HD)] = (mine * totals[i]).astype(out_ref.dtype)
            else:
                acc[index, rows, :] = mine

    whole, near_only, far_only = range(pairs), range(1), range(1, pairs)
    every_c, later_c = range(kv_heads), range(1, kv_heads)

    def of(k, s, ds):
        return [(k, s, d) for d in ds]

    def near(cs, units):
        for c in cs:
            absorb(pair * unit_keys, unit_keys, c, units)

    def far_rows(c, units):
        if pairs == 2:
            absorb((1 - pair) * unit_keys, unit_keys, c, units)
        else:
            def run(d, carry):
                absorb(lax.rem(pair + d, pairs) * unit_keys, unit_keys, c, units)
                return carry

            lax.fori_loop(1, pairs, run, 0)

    def full(cs, units, final=False):
        for c in cs:
            absorb(0, shard, c, units, final)

    def looped(run):
        def step(c, carry):
            run(c)
            return carry

        lax.fori_loop(0, kv_heads, step, 0)

    own = of(0, parity, whole)
    beside = of(0, other, whole)
    below = of(1, parity, whole)
    third = of(1, other, near_only) + of(2, parity, near_only)
    fourth = of(2, parity, far_only) + of(2, other, near_only)
    fifth = of(2, other, far_only) + of(3, parity, whole)
    sixth = of(1, other, far_only) + of(3, other, near_only)
    last = of(3, other, far_only)

    def both_parities(cond, run):
        @pl.when((parity == 1) & cond)
        def _():
            run(beside + below)

        @pl.when((parity == 0) & cond)
        def _():
            run(below)

    def climbed(k, ds):
        if k > hops:
            return

        @pl.when((level >= k) & by_parity(lambda p: climbs(k, p)))
        def _():
            for d in ds:
                for m in range(2):
                    push(k - 1, d, m).wait_recv()

                    @pl.when(up & by_parity(lambda p: climbs(k + 1, p)))
                    def _():
                        push(k, d, m).start()

                    @pl.when(by_parity(lambda p: crosses(k, p) and not (k == 1 and d >= 1 and p == 0)))
                    def _():
                        share(k, d, m).start()

    def crossed(k, ds):
        if k > hops:
            return
        for d in ds:
            @pl.when((level >= k) & by_parity(lambda p: crosses(k, 1 - p) and not (k == 1 and d >= 1 and p == 1)))
            def _():
                for m in range(2):
                    share(k, d, m).wait_recv()

            if k == 1 and d >= 1:
                @pl.when(down & (parity == 1))
                def _():
                    for m in range(2):
                        lift(d, m).wait_recv()

    for which in range(2):
        raw_own(which).wait()
        raw_mate(which).wait_recv()
    for d in far_only:
        for m in range(2):
            mine = half(0, parity, d, m)
            remote(mine, mine, far_send.at[d, 0, 0], far_recv.at[d, m], t, mate).wait_recv()

            @pl.when(up)
            def _():
                push(0, d, m).start()

            @pl.when(parity == 0)
            def _():
                share(0, d, m).start()
    climbed(1, near_only)
    for c in range(kv_heads):
        q_own(c).wait()
        q_mate(c).wait_recv()
    near(every_c, own)
    climbed(1, far_only)
    crossed(0, whole)
    both_parities(down, lambda units: near(every_c, units))

    @pl.when((parity == 1) & (level == 0))
    def _():
        looped(lambda c: absorb(pair * unit_keys, unit_keys, c, beside))

    climbed(2, near_only)

    def await_q(c):
        for d in far_only:
            block = q_buf.at[c, column(lax.rem(pair + d, pairs) * unit_keys, unit_keys), :]
            remote(block, block, q_send.at[d, 0, c], q_recv.at[d, c], t, mate).wait_recv()

    await_q(0)
    high = level >= 2

    def start_far(c, units):
        far_rows(c, own)
        far_rows(c, units)

    both_parities(high, functools.partial(start_far, 0))
    crossed(1, near_only)

    @pl.when(high)
    def _():
        full(range(1), third)
        near(later_c, third)

    climbed(2, far_only)

    @pl.when(up & (parity == 1))
    def _():
        for d in far_only:
            for m in range(2):
                lift(d, m).start()

    crossed(2, near_only)

    @pl.when(high)
    def _():
        full(range(1), fourth)
        near(later_c, fourth)

    climbed(3, near_only)
    for c in later_c:
        await_q(c)

        def rest(units):
            start_far(c, units)
            far_rows(c, third + fourth)

        both_parities(high, rest)

    @pl.when(level < 2)
    def _():
        looped(lambda c: far_rows(c, own))

    both_parities(level == 1, lambda units: looped(lambda c: far_rows(c, units)))

    @pl.when((parity == 1) & (level == 0))
    def _():
        looped(lambda c: far_rows(c, beside))

    climbed(3, far_only)
    crossed(2, far_only)
    deep = level >= 3
    if hops >= 3:
        @pl.when(deep)
        def _():
            full(every_c, fifth)
    climbed(4, whole)
    crossed(3, near_only)
    crossed(1, far_only)
    if hops >= 3:
        @pl.when(deep)
        def _():
            full(every_c, sixth)
    crossed(3, far_only)
    fused = hops == 3
    if hops >= 3:
        @pl.when(deep)
        def _():
            full(every_c, last, final=fused)

    @pl.when((level == 2) if hops >= 3 else high)
    def _():
        looped(lambda c: absorb(0, shard, c, of(1, other, far_only) + of(2, other, far_only)))

    @pl.when(level == 1)
    def _():
        looped(lambda c: absorb(0, shard, c, of(1, other, whole)))

    crossed(4, whole)
    if hops >= 4:
        @pl.when((level >= 4) & (parity == 0))
        def _():
            looped(lambda c: absorb(0, shard, c, of(4, 1, whole)))

    def finish(index, carry):
        total = jnp.sum(part[index], axis=1, keepdims=True)
        result = (acc[index] * (1.0 / total)).astype(out_ref.dtype)
        out_ref[:, pl.ds(pl.multiple_of(index * HD, HD), HD)] = result
        return carry

    @pl.when(level < (3 if fused else levels))
    def _():
        lax.fori_loop(0, kv_heads * GROUPS, finish, 0, unroll=2)

    for d, m in far:
        for which in range(2):
            raw_far(d, m, which).wait_send()
        for c in range(kv_heads):
            q_far(d, m, c).wait_send()
    for which in range(2):
        raw_mate(which).wait_send()
    for c in range(kv_heads):
        q_mate(c).wait_send()

    @pl.when(up)
    def _():
        for i in range(2):
            for which in range(2):
                raw_z(i, which).wait_send()
        for d in far_only:
            for m in range(2):
                push(0, d, m).wait_send()

    @pl.when(parity == 0)
    def _():
        for i in range(2):
            for which in range(2):
                raw_x(i, which).wait_send()
        for d in far_only:
            for m in range(2):
                share(0, d, m).wait_send()

    @pl.when(up & (parity == 1))
    def _():
        for d in far_only:
            for m in range(2):
                lift(d, m).wait_send()
    for k in range(1, hops + 1):
        @pl.when((level >= k) & by_parity(lambda p: climbs(k, p)))
        def _():
            for d in whole:
                for m in range(2):
                    @pl.when(up & by_parity(lambda p: climbs(k + 1, p)))
                    def _():
                        push(k, d, m).wait_send()

                    @pl.when(by_parity(lambda p: crosses(k, p) and not (k == 1 and d >= 1 and p == 0)))
                    def _():
                        share(k, d, m).wait_send()


def body(queries, keys, values, doc_ids):
    tok_len, head_len = lax.axis_size("tok"), lax.axis_size("head")
    piece = queries.shape[0]
    shard = piece * head_len
    kv_heads = KVH // head_len
    pairs = head_len // 2
    wide = GROUPS * HD
    hops = min((REACH + 1) // 2, tok_len // 2 - 1)
    heads = kv_heads * GROUPS
    lanes = min(HD, 2 * piece)
    DMA = pltpu.SemaphoreType.DMA
    anywhere = pl.BlockSpec(memory_space=pl.ANY)
    vmem = pl.BlockSpec(memory_space=pltpu.VMEM)
    return pl.pallas_call(
        functools.partial(kernel, tok_len, head_len, hops),
        out_shape=pltpu.VMEM((shard, heads * HD), jnp.bfloat16),
        in_specs=[anywhere] * 4,
        out_specs=vmem,
        scratch_shapes=[
            pltpu.VMEM((1, doc_ids.shape[0]), jnp.int32),
            pltpu.VMEM((kv_heads, shard, wide), jnp.bfloat16),
            pltpu.VMEM((2 * (hops + 1), pairs, 4, piece, kv_heads * HD), jnp.bfloat16),
            pltpu.VMEM((2 * (hops + 1), pairs, shard, 2 * piece), jnp.float32),
            pltpu.VMEM((heads, shard, HD), jnp.float32),
            pltpu.VMEM((heads, shard, lanes), jnp.float32),
            pltpu.VMEM((heads, shard, HD), jnp.float32),
            DMA((2,)),
            DMA((kv_heads,)),
            DMA((2,)),
            DMA((2,)),
            DMA((pairs, 2, 2)),
            DMA((pairs, 2)),
            DMA((pairs, 2, kv_heads)),
            DMA((pairs, kv_heads)),
            DMA((2, 2)),
            DMA((2, 2)),
            DMA((hops + 2, pairs, 2)),
            DMA((hops + 2, pairs, 2)),
            DMA((hops + 1, pairs, 2)),
            DMA((hops + 1, pairs, 2)),
            DMA((pairs, 2)),
            DMA((pairs, 2)),
            DMA,
            pltpu.SemaphoreType.REGULAR,
        ],
        compiler_params=pltpu.CompilerParams(
            collective_id=0, has_side_effects=True, vmem_limit_bytes=32 * 1000 * 1000
        ),
    )(*(pltpu.with_memory_space_constraint(a, pltpu.HBM) for a in (queries, keys, values, doc_ids.reshape(1, -1))))


def solution(mesh):
    return jax.shard_map(
        body,
        mesh=mesh,
        in_specs=(
            P(("tok", "head"), None),
            P(("tok", "head"), None),
            P(("tok", "head"), None),
            P(),
        ),
        out_specs=P("tok", "head"),
        check_vma=False,
    )
```

```python
import functools

import jax
import jax.numpy as jnp
from jax import lax
from jax.experimental import pallas as pl
from jax.experimental.pallas import tpu as pltpu
from jax.sharding import PartitionSpec as P

QH = 64
KVH = 8
HD = 128
REACH = 7
GROUPS = QH // KVH
MESH = pl.DeviceIdType.MESH
NEG = -1e30
LOWEST = -3e38
SCALE = HD ** -0.5 * 1.4426950408889634


def kernel(
    tok_len, head_len, hops,
    q_hbm, k_hbm, v_hbm, ids_hbm, out_ref,
    ids_ref, q_buf, kv, bias, peak, part, acc,
    own_sem, q_own_sem, mate_send, mate_recv, far_send, far_recv, q_send, q_recv,
    raw_z_send, raw_x_send, z_send, z_recv, x_send, x_recv, lift_send, lift_recv, ids_sem, ready,
):
    t, h = lax.axis_index("tok"), lax.axis_index("head")
    level, parity = t // 2, lax.rem(t, 2)
    pair, member = h // 2, lax.rem(h, 2)
    other = 1 - parity
    partner, mate = level * 2 + other, pair * 2 + (1 - member)
    levels, pairs = tok_len // 2, head_len // 2
    piece = q_hbm.shape[0]
    kv_heads, shard, wide = q_buf.shape
    q_cols, kv_cols = kv_heads * wide, kv_heads * HD
    unit_keys = 2 * piece
    lanes = part.shape[2]
    sources = (k_hbm, v_hbm)
    up, down = level + 1 < levels, level >= 1

    def by_parity(rule):
        return parity * int(rule(1)) + (1 - parity) * int(rule(0)) == 1

    def climbs(k, p):
        return k <= hops and (2 * k <= REACH or 2 * k + 1 - 2 * p <= REACH)

    def crosses(k, p):
        return k <= hops and 0 <= 2 * k + 1 - 2 * p <= REACH

    def column(start, size):
        return pl.ds(pl.multiple_of(start, size), size)

    def half(k, s, d, m):
        return kv.at[2 * k + s, lax.rem(pair + d, pairs), pl.ds(2 * m, 2)]

    def remote(src, dst, send, recv, tok, head):
        return pltpu.make_async_remote_copy(
            src_ref=src, dst_ref=dst, send_sem=send, recv_sem=recv,
            device_id={"tok": tok, "head": head}, device_id_type=MESH,
        )

    def raw(g, which):
        return sources[which].at[:, column(g * kv_cols, kv_cols)]

    def place(k, s, which):
        return kv.at[2 * k + s, pair, 2 * member + which]

    def raw_z(i, which):
        g = (h, mate)[i]
        return remote(raw(g, which), place(1, parity, which), raw_z_send.at[i, which], z_recv.at[1, 0, member], t + 2, g)

    def raw_x(i, which):
        g = (h, mate)[i]
        return remote(raw(g, which), place(0, 0, which), raw_x_send.at[i, which], x_recv.at[0, 0, member], partner, g)

    def raw_mate(which):
        return remote(raw(mate, which), place(0, parity, which), mate_send.at[which], mate_recv.at[which], t, mate)

    def raw_own(which):
        return pltpu.make_async_copy(raw(h, which), place(0, parity, which), own_sem.at[which])

    def raw_far(d, m, which):
        g = lax.rem(pair + d, pairs) * 2 + m
        return remote(raw(g, which), place(0, parity, which), far_send.at[d, m, which], far_recv.at[pairs - d, member], t, g)

    def q_rows(hh, c):
        return q_buf.at[c, pl.ds(pl.multiple_of(hh * piece, piece), piece), :]

    def q_cols_of(g, c):
        return q_hbm.at[:, column(g * q_cols + c * wide, wide)]

    def q_far(d, m, c):
        g = lax.rem(pair + d, pairs) * 2 + m
        return remote(q_cols_of(g, c), q_rows(h, c), q_send.at[d, m, c], q_recv.at[pairs - d, c], t, g)

    def q_mate(c):
        return remote(q_cols_of(mate, c), q_rows(h, c), q_send.at[0, 0, c], q_recv.at[0, c], t, mate)

    def q_own(c):
        return pltpu.make_async_copy(q_cols_of(h, c), q_rows(h, c), q_own_sem.at[c])

    def push(k, d, m):
        return remote(
            half(k, parity, d, m), half(k + 1, parity, d, m), z_send.at[k + 1, d, m], z_recv.at[k + 1, d, m], t + 2, h
        )

    def share(k, d, m):
        return remote(half(k, parity, d, m), half(k, parity, d, m), x_send.at[k, d, m], x_recv.at[k, d, m], partner, h)

    def lift(d, m):
        return remote(half(0, 0, d, m), half(1, 0, d, m), lift_send.at[d, m], lift_recv.at[d, m], t + 2, h)

    ids_copy = pltpu.make_async_copy(ids_hbm, ids_ref, ids_sem)
    ids_copy.start()
    for which in range(2):
        raw_own(which).start()
    for c in range(kv_heads):
        q_own(c).start()

    barrier = pltpu.get_barrier_semaphore()

    def greet(tok, head):
        pl.semaphore_signal(barrier, inc=1, device_id={"tok": tok, "head": head}, device_id_type=MESH)

    greet(t, mate)
    for p in range(1, pairs):
        @pl.when(p > pair)
        def _():
            for m in range(2):
                greet(t, 2 * p + m)

    for g in (h, mate):
        @pl.when(parity == 0)
        def _():
            greet(partner, g)

        @pl.when(up)
        def _():
            greet(t + 2, g)
    pl.semaphore_wait(barrier, 1 + 2 * pair + 2 * parity + 2 * jnp.minimum(level, 1))

    def answer(sem, tok, head):
        pl.semaphore_signal(sem, inc=1, device_id={"tok": tok, "head": head}, device_id_type=MESH)

    for p in range(pairs - 1):
        @pl.when(p < pair)
        def _():
            for m in range(2):
                answer(ready.at[1], t, 2 * p + m)

    for g in (h, mate):
        @pl.when(parity == 1)
        def _():
            answer(ready.at[2], partner, g)

        @pl.when(down)
        def _():
            answer(ready.at[0], t - 2, g)

    for which in range(2):
        raw_mate(which).start()
    for c in range(kv_heads):
        q_mate(c).start()
    far = [(d, m) for d in range(1, pairs) for m in range(2)]
    by_core = (member, 1 - member)

    @pl.when(pair < pairs - 1)
    def _():
        pl.semaphore_wait(ready.at[1], 2 * (pairs - 1 - pair))
    for m in by_core:
        for d in range(1, pairs):
            for which in range(2):
                raw_far(d, m, which).start()

    @pl.when(parity == 0)
    def _():
        pl.semaphore_wait(ready.at[2], 2)
        for i in range(2):
            for which in range(2):
                raw_x(i, which).start()
    for c in range(kv_heads):
        for d, m in far:
            q_far(d, m, c).start()

    @pl.when(up)
    def _():
        pl.semaphore_wait(ready.at[0], 2)
        for i in range(2):
            for which in range(2):
                raw_z(i, which).start()

    ids_copy.wait()

    own_ids = ids_ref[:, column(t * shard, shard)]
    id_column = jnp.broadcast_to(own_ids, (shard, shard)).T
    q_pos = t * shard + lax.broadcasted_iota(jnp.int32, (shard, shard), 0)
    k_iota = lax.broadcasted_iota(jnp.int32, (shard, shard), 1)
    for k in range(hops + 1):
        @pl.when(level >= k)
        def _():
            for s in range(2):
                start = ((level - k) * 2 + s) * shard
                key_ids = ids_ref[:, column(start, shard)]
                visible = (id_column == key_ids) & (start + k_iota <= q_pos)
                shown = jnp.where(visible, 0.0, NEG)
                for p in range(pairs):
                    bias[2 * k + s, p] = shown[:, p * unit_keys:(p + 1) * unit_keys]

    def clear(i, carry):
        peak[i] = jnp.full((shard, HD), LOWEST, jnp.float32)
        part[i] = jnp.zeros((shard, lanes), jnp.float32)
        acc[i] = jnp.zeros((shard, HD), jnp.float32)
        return carry

    lax.fori_loop(0, kv_heads * GROUPS, clear, 0)

    def absorb(row, size, c, units, final=False):
        heads = pl.ds(pl.multiple_of(c * HD, HD), HD)
        rows = pl.ds(pl.multiple_of(row, piece), size)
        spots = [(2 * k + s, lax.rem(pair + d, pairs)) for k, s, d in units]

        def gather(which):
            return jnp.concatenate([kv[a, b, 2 * m + which, :, heads] for a, b in spots for m in range(2)], axis=0)

        q = jnp.concatenate([q_buf[c, rows, i * HD:(i + 1) * HD] for i in range(GROUPS)], axis=0)
        scores = lax.dot_general(
            q, gather(0), (((1,), (1,)), ((), ())), preferred_element_type=jnp.float32
        )
        rounded, decays, totals = [], [], []
        for i in range(GROUPS):
            index = c * GROUPS + i
            tiles = []
            for n, (a, b) in enumerate(spots):
                mine = scores[i * size:(i + 1) * size, n * unit_keys:(n + 1) * unit_keys]
                mine = mine * SCALE + bias[a, b, rows, :]
                tiles += [mine[:, x:x + lanes] for x in range(0, unit_keys, lanes)]
            top = functools.reduce(jnp.maximum, tiles)
            top = jnp.broadcast_to(jnp.max(top, axis=1, keepdims=True), (size, HD))
            before = peak[index, rows, :]
            top = jnp.maximum(before, top)
            decay = jnp.exp2(before - top)
            decays.append(decay)
            weights = [jnp.exp2(tile - top[:, :lanes]) for tile in tiles]
            total = part[index, rows, :] * decay[:, :lanes] + functools.reduce(jnp.add, weights)
            if final:
                totals.append(1.0 / jnp.sum(total, axis=1, keepdims=True))
            else:
                peak[index, rows, :] = top
                part[index, rows, :] = total
            rounded.append(jnp.concatenate([w.astype(jnp.bfloat16) for w in weights], axis=1))
        update = jnp.dot(jnp.concatenate(rounded, axis=0), gather(1), preferred_element_type=jnp.float32)
        for i in range(GROUPS):
            index = c * GROUPS + i
            mine = acc[index, rows, :] * decays[i] + update[i * size:(i + 1) * size]
            if final:
                out_ref[rows, column(index * HD, HD)] = (mine * totals[i]).astype(out_ref.dtype)
            else:
                acc[index, rows, :] = mine

    whole, near_only, far_only = range(pairs), range(1), range(1, pairs)
    every_c, later_c = range(kv_heads), range(1, kv_heads)

    def of(k, s, ds):
        return [(k, s, d) for d in ds]

    def near(cs, units):
        for c in cs:
            absorb(pair * unit_keys, unit_keys, c, units)

    def far_rows(c, units):
        if pairs == 2:
            absorb((1 - pair) * unit_keys, unit_keys, c, units)
        else:
            def run(d, carry):
                absorb(lax.rem(pair + d, pairs) * unit_keys, unit_keys, c, units)
                return carry

            lax.fori_loop(1, pairs, run, 0)

    def full(cs, units, final=False):
        for c in cs:
            absorb(0, shard, c, units, final)

    def looped(run):
        def step(c, carry):
            run(c)
            return carry

        lax.fori_loop(0, kv_heads, step, 0)

    own = of(0, parity, whole)
    beside = of(0, other, whole)
    below = of(1, parity, whole)
    third = of(1, other, near_only) + of(2, parity, near_only)
    fourth = of(2, parity, far_only) + of(2, other, near_only)
    fifth = of(2, other, far_only) + of(3, parity, whole)
    sixth = of(1, other, far_only) + of(3, other, near_only)
    last = of(3, other, far_only)

    def both_parities(cond, run):
        @pl.when((parity == 1) & cond)
        def _():
            run(beside + below)

        @pl.when((parity == 0) & cond)
        def _():
            run(below)

    def climbed(k, ds, where=True):
        if k > hops:
            return

        @pl.when((level >= k) & by_parity(lambda p: climbs(k, p)) & where)
        def _():
            for d in ds:
                for m in range(2):
                    push(k - 1, d, m).wait_recv()

                    @pl.when(up & by_parity(lambda p: climbs(k + 1, p)))
                    def _():
                        push(k, d, m).start()

                    @pl.when(by_parity(lambda p: crosses(k, p) and not (k == 1 and d >= 1 and p == 0)))
                    def _():
                        share(k, d, m).start()

    def crossed(k, ds):
        if k > hops:
            return
        for d in ds:
            @pl.when((level >= k) & by_parity(lambda p: crosses(k, 1 - p) and not (k == 1 and d >= 1 and p == 1)))
            def _():
                for m in range(2):
                    share(k, d, m).wait_recv()

            if k == 1 and d >= 1:
                @pl.when(down & (parity == 1))
                def _():
                    for m in range(2):
                        lift(d, m).wait_recv()

    for which in range(2):
        raw_own(which).wait()
        raw_mate(which).wait_recv()
    sends_own = up | (parity == 0)
    climbed(1, near_only, jnp.logical_not(sends_own))
    for m in by_core:
        for d in far_only:
            mine = half(0, parity, d, m)
            remote(mine, mine, far_send.at[d, 0, 0], far_recv.at[d, m], t, mate).wait_recv()

            @pl.when(up)
            def _():
                push(0, d, m).start()

            @pl.when(parity == 0)
            def _():
                share(0, d, m).start()
    climbed(1, near_only, sends_own)
    for c in range(kv_heads):
        q_own(c).wait()
        q_mate(c).wait_recv()
    near(every_c, own)
    climbed(1, far_only)
    crossed(0, whole)
    both_parities(down, lambda units: near(every_c, units))

    @pl.when((parity == 1) & (level == 0))
    def _():
        looped(lambda c: absorb(pair * unit_keys, unit_keys, c, beside))

    climbed(2, near_only)

    def await_q(c):
        for d in far_only:
            block = q_buf.at[c, column(lax.rem(pair + d, pairs) * unit_keys, unit_keys), :]
            remote(block, block, q_send.at[d, 0, c], q_recv.at[d, c], t, mate).wait_recv()

    await_q(0)
    high = level >= 2

    def start_far(c, units):
        far_rows(c, own)
        far_rows(c, units)

    both_parities(high, functools.partial(start_far, 0))
    crossed(1, near_only)

    @pl.when(high)
    def _():
        full(range(1), third)
        near(later_c, third)

    climbed(2, far_only)

    @pl.when(up & (parity == 1))
    def _():
        for d in far_only:
            for m in range(2):
                lift(d, m).start()

    crossed(2, near_only)

    @pl.when(high)
    def _():
        full(range(1), fourth)
        near(later_c, fourth)

    climbed(3, near_only)
    for c in later_c:
        await_q(c)

        def rest(units):
            start_far(c, units)
            far_rows(c, third + fourth)

        both_parities(high, rest)

    @pl.when(level < 2)
    def _():
        looped(lambda c: far_rows(c, own))

    both_parities(level == 1, lambda units: looped(lambda c: far_rows(c, units)))

    @pl.when((parity == 1) & (level == 0))
    def _():
        looped(lambda c: far_rows(c, beside))

    climbed(3, far_only)
    crossed(2, far_only)
    deep = level >= 3
    if hops >= 3:
        @pl.when(deep)
        def _():
            full(every_c, fifth)
    climbed(4, whole)
    crossed(3, near_only)
    crossed(1, far_only)
    if hops >= 3:
        @pl.when(deep)
        def _():
            full(every_c, sixth)
    crossed(3, far_only)
    fused = hops == 3
    if hops >= 3:
        @pl.when(deep)
        def _():
            full(every_c, last, final=fused)

    @pl.when((level == 2) if hops >= 3 else high)
    def _():
        looped(lambda c: absorb(0, shard, c, of(1, other, far_only) + of(2, other, far_only)))

    @pl.when(level == 1)
    def _():
        looped(lambda c: absorb(0, shard, c, of(1, other, whole)))

    crossed(4, whole)
    if hops >= 4:
        @pl.when((level >= 4) & (parity == 0))
        def _():
            looped(lambda c: absorb(0, shard, c, of(4, 1, whole)))

    def finish(index, carry):
        total = jnp.sum(part[index], axis=1, keepdims=True)
        result = (acc[index] * (1.0 / total)).astype(out_ref.dtype)
        out_ref[:, pl.ds(pl.multiple_of(index * HD, HD), HD)] = result
        return carry

    @pl.when(level < (3 if fused else levels))
    def _():
        lax.fori_loop(0, kv_heads * GROUPS, finish, 0, unroll=2)

    for d, m in far:
        for which in range(2):
            raw_far(d, m, which).wait_send()
        for c in range(kv_heads):
            q_far(d, m, c).wait_send()
    for which in range(2):
        raw_mate(which).wait_send()
    for c in range(kv_heads):
        q_mate(c).wait_send()

    @pl.when(up)
    def _():
        for i in range(2):
            for which in range(2):
                raw_z(i, which).wait_send()
        for d in far_only:
            for m in range(2):
                push(0, d, m).wait_send()

    @pl.when(parity == 0)
    def _():
        for i in range(2):
            for which in range(2):
                raw_x(i, which).wait_send()
        for d in far_only:
            for m in range(2):
                share(0, d, m).wait_send()

    @pl.when(up & (parity == 1))
    def _():
        for d in far_only:
            for m in range(2):
                lift(d, m).wait_send()
    for k in range(1, hops + 1):
        @pl.when((level >= k) & by_parity(lambda p: climbs(k, p)))
        def _():
            for d in whole:
                for m in range(2):
                    @pl.when(up & by_parity(lambda p: climbs(k + 1, p)))
                    def _():
                        push(k, d, m).wait_send()

                    @pl.when(by_parity(lambda p: crosses(k, p) and not (k == 1 and d >= 1 and p == 0)))
                    def _():
                        share(k, d, m).wait_send()


def body(queries, keys, values, doc_ids):
    tok_len, head_len = lax.axis_size("tok"), lax.axis_size("head")
    piece = queries.shape[0]
    shard = piece * head_len
    kv_heads = KVH // head_len
    pairs = head_len // 2
    wide = GROUPS * HD
    hops = min((REACH + 1) // 2, tok_len // 2 - 1)
    heads = kv_heads * GROUPS
    lanes = min(HD, 2 * piece)
    DMA = pltpu.SemaphoreType.DMA
    anywhere = pl.BlockSpec(memory_space=pl.ANY)
    vmem = pl.BlockSpec(memory_space=pltpu.VMEM)
    return pl.pallas_call(
        functools.partial(kernel, tok_len, head_len, hops),
        out_shape=pltpu.VMEM((shard, heads * HD), jnp.bfloat16),
        in_specs=[anywhere] * 4,
        out_specs=vmem,
        scratch_shapes=[
            pltpu.VMEM((1, doc_ids.shape[0]), jnp.int32),
            pltpu.VMEM((kv_heads, shard, wide), jnp.bfloat16),
            pltpu.VMEM((2 * (hops + 1), pairs, 4, piece, kv_heads * HD), jnp.bfloat16),
            pltpu.VMEM((2 * (hops + 1), pairs, shard, 2 * piece), jnp.float32),
            pltpu.VMEM((heads, shard, HD), jnp.float32),
            pltpu.VMEM((heads, shard, lanes), jnp.float32),
            pltpu.VMEM((heads, shard, HD), jnp.float32),
            DMA((2,)),
            DMA((kv_heads,)),
            DMA((2,)),
            DMA((2,)),
            DMA((pairs, 2, 2)),
            DMA((pairs, 2)),
            DMA((pairs, 2, kv_heads)),
            DMA((pairs, kv_heads)),
            DMA((2, 2)),
            DMA((2, 2)),
            DMA((hops + 2, pairs, 2)),
            DMA((hops + 2, pairs, 2)),
            DMA((hops + 1, pairs, 2)),
            DMA((hops + 1, pairs, 2)),
            DMA((pairs, 2)),
            DMA((pairs, 2)),
            DMA,
            pltpu.SemaphoreType.REGULAR((3,)),
        ],
        compiler_params=pltpu.CompilerParams(
            collective_id=0, has_side_effects=True, vmem_limit_bytes=32 * 1000 * 1000
        ),
    )(*(pltpu.with_memory_space_constraint(a, pltpu.HBM) for a in (queries, keys, values, doc_ids.reshape(1, -1))))


def solution(mesh):
    return jax.shard_map(
        body,
        mesh=mesh,
        in_specs=(
            P(("tok", "head"), None),
            P(("tok", "head"), None),
            P(("tok", "head"), None),
            P(),
        ),
        out_specs=P("tok", "head"),
        check_vma=False,
    )
```

```python
import functools

import jax
import jax.numpy as jnp
from jax import lax
from jax.experimental import pallas as pl
from jax.experimental.pallas import tpu as pltpu
from jax.sharding import PartitionSpec as P

QH = 64
KVH = 8
HD = 128
REACH = 7
GROUPS = QH // KVH
MESH = pl.DeviceIdType.MESH
NEG = -1e30
LOWEST = -3e38
SCALE = HD ** -0.5 * 1.4426950408889634


def kernel(
    tok_len, head_len, hops,
    q_hbm, k_hbm, v_hbm, ids_hbm, out_ref,
    ids_ref, q_buf, kv, bias, peak, part, acc,
    own_sem, q_own_sem, mate_send, mate_recv, far_send, far_recv, q_send, q_recv,
    raw_z_send, raw_x_send, z_send, z_recv, x_send, x_recv, lift_send, lift_recv, ids_sem, ready,
):
    t, h = lax.axis_index("tok"), lax.axis_index("head")
    level, parity = t // 2, lax.rem(t, 2)
    pair, member = h // 2, lax.rem(h, 2)
    other = 1 - parity
    partner, mate = level * 2 + other, pair * 2 + (1 - member)
    levels, pairs = tok_len // 2, head_len // 2
    piece = q_hbm.shape[0]
    kv_heads, shard, wide = q_buf.shape
    q_cols, kv_cols = kv_heads * wide, kv_heads * HD
    unit_keys = 2 * piece
    lanes = part.shape[2]
    sources = (k_hbm, v_hbm)
    up, down = level + 1 < levels, level >= 1

    def by_parity(rule):
        return parity * int(rule(1)) + (1 - parity) * int(rule(0)) == 1

    def climbs(k, p):
        return k <= hops and (2 * k <= REACH or 2 * k + 1 - 2 * p <= REACH)

    def crosses(k, p):
        return k <= hops and 0 <= 2 * k + 1 - 2 * p <= REACH

    def column(start, size):
        return pl.ds(pl.multiple_of(start, size), size)

    def half(k, s, d, m):
        return kv.at[2 * k + s, lax.rem(pair + d, pairs), pl.ds(2 * m, 2)]

    def remote(src, dst, send, recv, tok, head):
        return pltpu.make_async_remote_copy(
            src_ref=src, dst_ref=dst, send_sem=send, recv_sem=recv,
            device_id={"tok": tok, "head": head}, device_id_type=MESH,
        )

    def raw(g, which):
        return sources[which].at[:, column(g * kv_cols, kv_cols)]

    def place(k, s, which):
        return kv.at[2 * k + s, pair, 2 * member + which]

    def raw_z(i, which):
        g = (h, mate)[i]
        return remote(raw(g, which), place(1, parity, which), raw_z_send.at[i, which], z_recv.at[1, 0, member], t + 2, g)

    def raw_x(i, which):
        g = (h, mate)[i]
        return remote(raw(g, which), place(0, 0, which), raw_x_send.at[i, which], x_recv.at[0, 0, member], partner, g)

    def raw_mate(which):
        return remote(raw(mate, which), place(0, parity, which), mate_send.at[which], mate_recv.at[which], t, mate)

    def raw_own(which):
        return pltpu.make_async_copy(raw(h, which), place(0, parity, which), own_sem.at[which])

    def raw_far(d, m, which):
        g = lax.rem(pair + d, pairs) * 2 + m
        return remote(raw(g, which), place(0, parity, which), far_send.at[d, m, which], far_recv.at[pairs - d, member], t, g)

    def q_rows(hh, c):
        return q_buf.at[c, pl.ds(pl.multiple_of(hh * piece, piece), piece), :]

    def q_cols_of(g, c):
        return q_hbm.at[:, column(g * q_cols + c * wide, wide)]

    def q_far(d, m, c):
        g = lax.rem(pair + d, pairs) * 2 + m
        return remote(q_cols_of(g, c), q_rows(h, c), q_send.at[d, m, c], q_recv.at[pairs - d, c], t, g)

    def q_mate(c):
        return remote(q_cols_of(mate, c), q_rows(h, c), q_send.at[0, 0, c], q_recv.at[0, c], t, mate)

    def q_own(c):
        return pltpu.make_async_copy(q_cols_of(h, c), q_rows(h, c), q_own_sem.at[c])

    def push(k, d, m):
        return remote(
            half(k, parity, d, m), half(k + 1, parity, d, m), z_send.at[k + 1, d, m], z_recv.at[k + 1, d, m], t + 2, h
        )

    def share(k, d, m):
        return remote(half(k, parity, d, m), half(k, parity, d, m), x_send.at[k, d, m], x_recv.at[k, d, m], partner, h)

    def lift(d, m):
        return remote(half(0, 0, d, m), half(1, 0, d, m), lift_send.at[d, m], lift_recv.at[d, m], t + 2, h)

    ids_copy = pltpu.make_async_copy(ids_hbm, ids_ref, ids_sem)
    ids_copy.start()
    for which in range(2):
        raw_own(which).start()
    for c in range(kv_heads):
        q_own(c).start()

    barrier = pltpu.get_barrier_semaphore()

    def greet(tok, head):
        pl.semaphore_signal(barrier, inc=1, device_id={"tok": tok, "head": head}, device_id_type=MESH)

    greet(t, mate)
    for p in range(1, pairs):
        @pl.when(p > pair)
        def _():
            for m in range(2):
                greet(t, 2 * p + m)

    for g in (h, mate):
        @pl.when(parity == 0)
        def _():
            greet(partner, g)

        @pl.when(up)
        def _():
            greet(t + 2, g)
    pl.semaphore_wait(barrier, 1 + 2 * pair + 2 * parity + 2 * jnp.minimum(level, 1))

    def answer(sem, tok, head):
        pl.semaphore_signal(sem, inc=1, device_id={"tok": tok, "head": head}, device_id_type=MESH)

    for p in range(pairs - 1):
        @pl.when(p < pair)
        def _():
            for m in range(2):
                answer(ready.at[1], t, 2 * p + m)

    for g in (h, mate):
        @pl.when(parity == 1)
        def _():
            answer(ready.at[2], partner, g)

        @pl.when(down)
        def _():
            answer(ready.at[0], t - 2, g)

    for which in range(2):
        raw_mate(which).start()
    for c in range(kv_heads):
        q_mate(c).start()
    far = [(d, m) for d in range(1, pairs) for m in range(2)]
    by_core = (member, 1 - member)

    @pl.when(pair < pairs - 1)
    def _():
        pl.semaphore_wait(ready.at[1], 2 * (pairs - 1 - pair))
    for m in by_core:
        for d in range(1, pairs):
            for which in range(2):
                raw_far(d, m, which).start()

    @pl.when(parity == 0)
    def _():
        pl.semaphore_wait(ready.at[2], 2)
        for i in range(2):
            for which in range(2):
                raw_x(i, which).start()
    for c in range(kv_heads):
        for d, m in far:
            q_far(d, m, c).start()

    @pl.when(up)
    def _():
        pl.semaphore_wait(ready.at[0], 2)
        for i in range(2):
            for which in range(2):
                raw_z(i, which).start()

    ids_copy.wait()

    own_ids = ids_ref[:, column(t * shard, shard)]
    id_column = jnp.broadcast_to(own_ids, (shard, shard)).T
    q_pos = t * shard + lax.broadcasted_iota(jnp.int32, (shard, shard), 0)
    k_iota = lax.broadcasted_iota(jnp.int32, (shard, shard), 1)
    for k in range(hops + 1):
        @pl.when(level >= k)
        def _():
            for s in range(2):
                start = ((level - k) * 2 + s) * shard
                key_ids = ids_ref[:, column(start, shard)]
                visible = (id_column == key_ids) & (start + k_iota <= q_pos)
                shown = jnp.where(visible, 0.0, NEG)
                for p in range(pairs):
                    bias[2 * k + s, p] = shown[:, p * unit_keys:(p + 1) * unit_keys]

    def clear(i, carry):
        peak[i] = jnp.full((shard, HD), LOWEST, jnp.float32)
        part[i] = jnp.zeros((shard, lanes), jnp.float32)
        acc[i] = jnp.zeros((shard, HD), jnp.float32)
        return carry

    lax.fori_loop(0, kv_heads * GROUPS, clear, 0)

    def absorb(row, size, c, units, final=False):
        heads = pl.ds(pl.multiple_of(c * HD, HD), HD)
        rows = pl.ds(pl.multiple_of(row, piece), size)
        spots = [(2 * k + s, lax.rem(pair + d, pairs)) for k, s, d in units]

        def gather(which):
            return jnp.concatenate([kv[a, b, 2 * m + which, :, heads] for a, b in spots for m in range(2)], axis=0)

        q = jnp.concatenate([q_buf[c, rows, i * HD:(i + 1) * HD] for i in range(GROUPS)], axis=0)
        scores = lax.dot_general(
            q, gather(0), (((1,), (1,)), ((), ())), preferred_element_type=jnp.float32
        )
        rounded, decays, totals = [], [], []
        for i in range(GROUPS):
            index = c * GROUPS + i
            tiles = []
            for n, (a, b) in enumerate(spots):
                mine = scores[i * size:(i + 1) * size, n * unit_keys:(n + 1) * unit_keys]
                mine = mine * SCALE + bias[a, b, rows, :]
                tiles += [mine[:, x:x + lanes] for x in range(0, unit_keys, lanes)]
            top = functools.reduce(jnp.maximum, tiles)
            top = jnp.broadcast_to(jnp.max(top, axis=1, keepdims=True), (size, HD))
            before = peak[index, rows, :]
            top = jnp.maximum(before, top)
            decay = jnp.exp2(before - top)
            decays.append(decay)
            weights = [jnp.exp2(tile - top[:, :lanes]) for tile in tiles]
            total = part[index, rows, :] * decay[:, :lanes] + functools.reduce(jnp.add, weights)
            if final:
                totals.append(1.0 / jnp.sum(total, axis=1, keepdims=True))
            else:
                peak[index, rows, :] = top
                part[index, rows, :] = total
            rounded.append(jnp.concatenate([w.astype(jnp.bfloat16) for w in weights], axis=1))
        update = jnp.dot(jnp.concatenate(rounded, axis=0), gather(1), preferred_element_type=jnp.float32)
        for i in range(GROUPS):
            index = c * GROUPS + i
            mine = acc[index, rows, :] * decays[i] + update[i * size:(i + 1) * size]
            if final:
                out_ref[rows, column(index * HD, HD)] = (mine * totals[i]).astype(out_ref.dtype)
            else:
                acc[index, rows, :] = mine

    whole, near_only, far_only = range(pairs), range(1), range(1, pairs)
    every_c, later_c = range(kv_heads), range(1, kv_heads)

    def of(k, s, ds):
        return [(k, s, d) for d in ds]

    def near(cs, units):
        for c in cs:
            absorb(pair * unit_keys, unit_keys, c, units)

    def far_rows(c, units):
        if pairs == 2:
            absorb((1 - pair) * unit_keys, unit_keys, c, units)
        else:
            def run(d, carry):
                absorb(lax.rem(pair + d, pairs) * unit_keys, unit_keys, c, units)
                return carry

            lax.fori_loop(1, pairs, run, 0)

    def full(cs, units, final=False):
        for c in cs:
            absorb(0, shard, c, units, final)

    def looped(run):
        def step(c, carry):
            run(c)
            return carry

        lax.fori_loop(0, kv_heads, step, 0)

    own = of(0, parity, whole)
    beside = of(0, other, whole)
    below = of(1, parity, whole)
    third = of(1, other, near_only) + of(2, parity, near_only)
    fourth = of(2, parity, far_only) + of(2, other, near_only)
    fifth = of(2, other, far_only) + of(3, parity, whole)
    sixth = of(1, other, far_only) + of(3, other, near_only)
    last = of(3, other, far_only)

    def both_parities(cond, run):
        @pl.when((parity == 1) & cond)
        def _():
            run(beside + below)

        @pl.when((parity == 0) & cond)
        def _():
            run(below)

    def climbed(k, ds, where=True):
        if k > hops:
            return

        @pl.when((level >= k) & by_parity(lambda p: climbs(k, p)) & where)
        def _():
            for d in ds:
                for m in by_core:
                    push(k - 1, d, m).wait_recv()

                    @pl.when(up & by_parity(lambda p: climbs(k + 1, p)))
                    def _():
                        push(k, d, m).start()

                    @pl.when(by_parity(lambda p: crosses(k, p) and not (k == 1 and d >= 1 and p == 0)))
                    def _():
                        share(k, d, m).start()

    def crossed(k, ds):
        if k > hops:
            return
        for d in ds:
            @pl.when((level >= k) & by_parity(lambda p: crosses(k, 1 - p) and not (k == 1 and d >= 1 and p == 1)))
            def _():
                for m in range(2):
                    share(k, d, m).wait_recv()

            if k == 1 and d >= 1:
                @pl.when(down & (parity == 1))
                def _():
                    for m in range(2):
                        lift(d, m).wait_recv()

    for which in range(2):
        raw_own(which).wait()
        raw_mate(which).wait_recv()
    sends_own = up | (parity == 0)
    climbed(1, near_only, jnp.logical_not(sends_own))
    for m in by_core:
        for d in far_only:
            mine = half(0, parity, d, m)
            remote(mine, mine, far_send.at[d, 0, 0], far_recv.at[d, m], t, mate).wait_recv()

            @pl.when(up)
            def _():
                push(0, d, m).start()

            @pl.when(parity == 0)
            def _():
                share(0, d, m).start()
    climbed(1, near_only, sends_own)
    for c in range(kv_heads):
        q_own(c).wait()
        q_mate(c).wait_recv()
    near(every_c, own)
    climbed(1, far_only)
    crossed(0, whole)
    both_parities(down, lambda units: near(every_c, units))

    @pl.when((parity == 1) & (level == 0))
    def _():
        looped(lambda c: absorb(pair * unit_keys, unit_keys, c, beside))

    climbed(2, near_only)

    def await_q(c):
        for d in far_only:
            block = q_buf.at[c, column(lax.rem(pair + d, pairs) * unit_keys, unit_keys), :]
            remote(block, block, q_send.at[d, 0, c], q_recv.at[d, c], t, mate).wait_recv()

    await_q(0)
    high = level >= 2

    def start_far(c, units):
        far_rows(c, own)
        far_rows(c, units)

    both_parities(high, functools.partial(start_far, 0))
    crossed(1, near_only)

    @pl.when(high)
    def _():
        full(range(1), third)
        near(later_c, third)

    climbed(2, far_only)

    @pl.when(up & (parity == 1))
    def _():
        for d in far_only:
            for m in range(2):
                lift(d, m).start()

    crossed(2, near_only)

    @pl.when(high)
    def _():
        full(range(1), fourth)
        near(later_c, fourth)

    climbed(3, near_only)
    for c in later_c:
        await_q(c)

        def rest(units):
            start_far(c, units)
            far_rows(c, third + fourth)

        both_parities(high, rest)

    @pl.when(level < 2)
    def _():
        looped(lambda c: far_rows(c, own))

    both_parities(level == 1, lambda units: looped(lambda c: far_rows(c, units)))

    @pl.when((parity == 1) & (level == 0))
    def _():
        looped(lambda c: far_rows(c, beside))

    climbed(3, far_only)
    crossed(2, far_only)
    deep = level >= 3
    if hops >= 3:
        @pl.when(deep)
        def _():
            full(every_c, fifth)
    climbed(4, whole)
    crossed(3, near_only)
    crossed(1, far_only)
    if hops >= 3:
        @pl.when(deep)
        def _():
            full(every_c, sixth)
    crossed(3, far_only)
    fused = hops == 3
    if hops >= 3:
        @pl.when(deep)
        def _():
            full(every_c, last, final=fused)

    @pl.when((level == 2) if hops >= 3 else high)
    def _():
        looped(lambda c: absorb(0, shard, c, of(1, other, far_only) + of(2, other, far_only)))

    @pl.when(level == 1)
    def _():
        looped(lambda c: absorb(0, shard, c, of(1, other, whole)))

    crossed(4, whole)
    if hops >= 4:
        @pl.when((level >= 4) & (parity == 0))
        def _():
            looped(lambda c: absorb(0, shard, c, of(4, 1, whole)))

    def finish(index, carry):
        total = jnp.sum(part[index], axis=1, keepdims=True)
        result = (acc[index] * (1.0 / total)).astype(out_ref.dtype)
        out_ref[:, pl.ds(pl.multiple_of(index * HD, HD), HD)] = result
        return carry

    @pl.when(level < (3 if fused else levels))
    def _():
        lax.fori_loop(0, kv_heads * GROUPS, finish, 0, unroll=2)

    for d, m in far:
        for which in range(2):
            raw_far(d, m, which).wait_send()
        for c in range(kv_heads):
            q_far(d, m, c).wait_send()
    for which in range(2):
        raw_mate(which).wait_send()
    for c in range(kv_heads):
        q_mate(c).wait_send()

    @pl.when(up)
    def _():
        for i in range(2):
            for which in range(2):
                raw_z(i, which).wait_send()
        for d in far_only:
            for m in range(2):
                push(0, d, m).wait_send()

    @pl.when(parity == 0)
    def _():
        for i in range(2):
            for which in range(2):
                raw_x(i, which).wait_send()
        for d in far_only:
            for m in range(2):
                share(0, d, m).wait_send()

    @pl.when(up & (parity == 1))
    def _():
        for d in far_only:
            for m in range(2):
                lift(d, m).wait_send()
    for k in range(1, hops + 1):
        @pl.when((level >= k) & by_parity(lambda p: climbs(k, p)))
        def _():
            for d in whole:
                for m in range(2):
                    @pl.when(up & by_parity(lambda p: climbs(k + 1, p)))
                    def _():
                        push(k, d, m).wait_send()

                    @pl.when(by_parity(lambda p: crosses(k, p) and not (k == 1 and d >= 1 and p == 0)))
                    def _():
                        share(k, d, m).wait_send()


def body(queries, keys, values, doc_ids):
    tok_len, head_len = lax.axis_size("tok"), lax.axis_size("head")
    piece = queries.shape[0]
    shard = piece * head_len
    kv_heads = KVH // head_len
    pairs = head_len // 2
    wide = GROUPS * HD
    hops = min((REACH + 1) // 2, tok_len // 2 - 1)
    heads = kv_heads * GROUPS
    lanes = min(HD, 2 * piece)
    DMA = pltpu.SemaphoreType.DMA
    anywhere = pl.BlockSpec(memory_space=pl.ANY)
    vmem = pl.BlockSpec(memory_space=pltpu.VMEM)
    return pl.pallas_call(
        functools.partial(kernel, tok_len, head_len, hops),
        out_shape=pltpu.VMEM((shard, heads * HD), jnp.bfloat16),
        in_specs=[anywhere] * 4,
        out_specs=vmem,
        scratch_shapes=[
            pltpu.VMEM((1, doc_ids.shape[0]), jnp.int32),
            pltpu.VMEM((kv_heads, shard, wide), jnp.bfloat16),
            pltpu.VMEM((2 * (hops + 1), pairs, 4, piece, kv_heads * HD), jnp.bfloat16),
            pltpu.VMEM((2 * (hops + 1), pairs, shard, 2 * piece), jnp.float32),
            pltpu.VMEM((heads, shard, HD), jnp.float32),
            pltpu.VMEM((heads, shard, lanes), jnp.float32),
            pltpu.VMEM((heads, shard, HD), jnp.float32),
            DMA((2,)),
            DMA((kv_heads,)),
            DMA((2,)),
            DMA((2,)),
            DMA((pairs, 2, 2)),
            DMA((pairs, 2)),
            DMA((pairs, 2, kv_heads)),
            DMA((pairs, kv_heads)),
            DMA((2, 2)),
            DMA((2, 2)),
            DMA((hops + 2, pairs, 2)),
            DMA((hops + 2, pairs, 2)),
            DMA((hops + 1, pairs, 2)),
            DMA((hops + 1, pairs, 2)),
            DMA((pairs, 2)),
            DMA((pairs, 2)),
            DMA,
            pltpu.SemaphoreType.REGULAR((3,)),
        ],
        compiler_params=pltpu.CompilerParams(
            collective_id=0, has_side_effects=True, vmem_limit_bytes=32 * 1000 * 1000
        ),
    )(*(pltpu.with_memory_space_constraint(a, pltpu.HBM) for a in (queries, keys, values, doc_ids.reshape(1, -1))))


def solution(mesh):
    return jax.shard_map(
        body,
        mesh=mesh,
        in_specs=(
            P(("tok", "head"), None),
            P(("tok", "head"), None),
            P(("tok", "head"), None),
            P(),
        ),
        out_specs=P("tok", "head"),
        check_vma=False,
    )
```
